32 devices in a mesh: gx: 4 (over y, x), gy: 8 (over z, core).
Axes of the slice: x: 2, y: 2, z: 4, core: 2. Of those that a mesh axis runs over, the one named last changes fastest.
Arguments:
- right_side: float32 [9, 128, 1024], P(None, 'gx', 'gy'), may hold values from -16 to 16
- diag_blocks: float32 [9, 9, 128, 1024], P(None, None, 'gx', 'gy'), may hold values from -0.3 to 6, as said below
- couple_blocks: float32 [9, 9, 128, 1024], P(None, None, 'gx', 'gy'), may hold values from -0.15 to 1.5, as said below
- transmissibility: float32 [4, 128, 1024], P(None, 'gx', 'gy'), may hold values from 0.1 to 0.8
- pressure_weights: float32 [9, 128, 1024], P(None, 'gx', 'gy'), may hold values from 0.2 to 1
- well_mask: int32 [128, 1024], P('gx', 'gy'), may hold values 0 or 1
Outputs:
- solution: float32 [9, 128, 1024], P(None, 'gx', 'gy')
- estimate: float32 [], replicated
The draws below stay inside these ranges and needn't reach their ends.
Inputs may be any that keep to these rules, and one draw needn't show every extreme that they name: `diag_blocks`: outside the first column, each block has diagonal entries from 4 to 6 and other entries within 0.3 in magnitude (within 0.05 in the first row); the first column is positive. `couple_blocks`: each block has first-column entries from 0.5 to 1.5, other diagonal entries from 0.6 to 1.2, and other entries within 0.15 in magnitude.
All inputs are finite; a program needn't handle non-finite values. No bound on the sum of `well_mask` on one device may be relied on, other than what follows from the above.
Results may differ from the reference program's by a relative error of at most 0.0003.
Values sent between devices are 32-bit elements; how exact they have to be, the bound alone decides.
A program may use at most 64 MiB of HBM per device.

```python
import math
import jax
import jax.numpy as jnp
from jax import lax

NC = 9
GSTEPS = 2
LEVELS = 3
COARSE_SWEEPS = 6
NX = 128
NY = 1024


def block_pattern(key, diag_low, diag_high, column_low, column_high, spread, column_first):
    array_shape = (NC, NC, NX, NY)
    key_off, key_column, key_diag = jax.random.split(key, 3)
    off_values = jax.random.uniform(key_off, array_shape, jnp.float32, -spread, spread)
    column_values = jax.random.uniform(key_column, array_shape, jnp.float32, column_low, column_high)
    diag_values = jax.random.uniform(key_diag, array_shape, jnp.float32, diag_low, diag_high)
    rows_iota = lax.broadcasted_iota(jnp.int32, array_shape, 0)
    cols_iota = lax.broadcasted_iota(jnp.int32, array_shape, 1)
    if column_first:
        return jnp.where(cols_iota == 0, column_values, jnp.where(rows_iota == cols_iota, diag_values, off_values))
    return jnp.where(rows_iota == cols_iota, diag_values, jnp.where(cols_iota == 0, column_values, off_values))


def flux_parts(key):
    trans_key = jax.random.fold_in(key, 101)
    log_values = jax.random.uniform(trans_key, (4, NX, NY), jnp.float32, math.log(0.1), math.log(0.8))
    face_trans = jnp.exp(log_values)
    couple = block_pattern(jax.random.fold_in(key, 23), 0.6, 1.2, 0.5, 1.5, 0.15, True)
    return (face_trans, couple)


def draw_transmissibility(key, part):
    return flux_parts(key)[0]


def draw_couple_blocks(key, part):
    return flux_parts(key)[1]


def draw_diag_blocks(key, part):
    face_trans, couple = flux_parts(key)
    array_shape = (NC, NC, NX, NY)
    key_off, key_diag, key_accum = jax.random.split(jax.random.fold_in(key, 11), 3)
    rows_iota = lax.broadcasted_iota(jnp.int32, array_shape, 0)
    cols_iota = lax.broadcasted_iota(jnp.int32, array_shape, 1)
    off_values = jax.random.uniform(key_off, array_shape, jnp.float32, -0.3, 0.3)
    off_values = jnp.where(rows_iota == 0, off_values / 6.0, off_values)
    diag_values = jax.random.uniform(key_diag, array_shape, jnp.float32, 4.0, 6.0)
    padded = jnp.pad(couple[:, 0], ((0, 0), (1, 1), (1, 1)))
    inflow = face_trans[0] * padded[:, 2:, 1:-1] + face_trans[1] * padded[:, :-2, 1:-1] + face_trans[2] * padded[:, 1:-1, 2:] + face_trans[3] * padded[:, 1:-1, :-2]
    accumulation = jax.random.uniform(key_accum, (NC, NX, NY), jnp.float32, 0.05, 0.15)
    first_column = (accumulation + inflow)[:, None]
    return jnp.where(cols_iota == 0, first_column, jnp.where(rows_iota == cols_iota, diag_values, off_values))


def draw_right_side(key, part):
    array_shape = (NC, NX, NY)
    key_rough = jax.random.fold_in(jax.random.fold_in(key, 37), 0)
    return jnp.clip(4.0 * jax.random.normal(key_rough, array_shape, jnp.float32), -16.0, 16.0)


def touch_ends(drawn, key, least, high):
    shape = drawn.shape
    spot = [jax.random.randint(jax.random.fold_in(key, axis), (), 0, shape[axis]) for axis in range(len(shape))]
    drawn = drawn.at[tuple(spot)].set(least)
    longest = shape.index(max(shape))
    spot[longest] = (spot[longest] + 1) % shape[longest]
    return drawn.at[tuple(spot)].set(high)


def block_scale(own_key, shape, pieces, smallest, top_value):
    factor_of = 1.0
    for position, parts in pieces:
        heights = jax.random.uniform(jax.random.fold_in(jax.random.fold_in(own_key, 6), position), (parts,), jnp.float32, smallest / len(pieces), top_value / len(pieces))
        factor_of = factor_of * jnp.repeat(jnp.exp(heights), shape[position] // parts).reshape((-1,) + (1,) * (len(shape) - 1 - position))
    return factor_of


def setup_inputs(seed: int = 0) -> dict:
    arg_keys = jax.random.split(jax.random.key(seed), 7)
    right_side = draw_right_side(jax.random.fold_in(arg_keys[6], 71), 0)
    diag_blocks = draw_diag_blocks(jax.random.fold_in(arg_keys[6], 71), 0)
    couple_blocks = draw_couple_blocks(jax.random.fold_in(arg_keys[6], 71), 0)
    transmissibility = draw_transmissibility(jax.random.fold_in(arg_keys[6], 71), 0)
    pressure_weights = jnp.clip(0.2 + 0.8 * jax.random.uniform(arg_keys[4], (NC, NX, NY), jnp.float32) ** block_scale(arg_keys[4], (NC, NX, NY), ((1, 4), (2, 8)), -0.2, 0.2), 0.2, 1.0)
    well_mask = touch_ends((jax.random.randint(arg_keys[5], (NX, NY), 0, 16) < 1).astype(jnp.int32), jax.random.fold_in(arg_keys[5], 1), 0, 1)
    return dict(right_side=right_side, diag_blocks=diag_blocks, couple_blocks=couple_blocks, transmissibility=transmissibility, pressure_weights=pressure_weights, well_mask=well_mask)


relax_factor = 0.8
well_boost = 8.0

def pad_cells(values):
    widths = [(0, 0)] * (values.ndim - 2) + [(1, 1), (1, 1)]
    return jnp.pad(values, widths)

def four_sides(padded):
    return (padded[..., 2:, 1:-1], padded[..., :-2, 1:-1], padded[..., 1:-1, 2:], padded[..., 1:-1, :-2])

def apply_blocks(vector, eff_diag, couple_blocks, face_trans, padder):
    product = lax.optimization_barrier(jnp.sum(couple_blocks * vector[None], axis=1))
    east_side, west_side, north_side, south_side = four_sides(padder(product))
    own_term = lax.optimization_barrier(jnp.sum(eff_diag * vector[None], axis=1))
    return own_term - (face_trans[0] * east_side + face_trans[1] * west_side + face_trans[2] * north_side + face_trans[3] * south_side)

def level_apply(values, coeffs, padder):
    east_side, west_side, north_side, south_side = four_sides(padder(values))
    return coeffs[0] * values + (coeffs[1] * east_side + coeffs[2] * west_side + coeffs[3] * north_side + coeffs[4] * south_side)

def jacobi_sweep(iterate, source, coeffs, padder):
    return iterate + relax_factor * (source - level_apply(iterate, coeffs, padder)) / coeffs[0]

def coarse_sweeps(source, coeffs, padder):
    iterate = relax_factor * source / coeffs[0]
    for sweep_no in range(COARSE_SWEEPS - 1):
        iterate = jacobi_sweep(iterate, source, coeffs, padder)
    return iterate

def coarsen(coeffs):
    extent_x, extent_y = (coeffs.shape[1], coeffs.shape[2])
    grouped = coeffs.reshape(5, extent_x // 2, 2, extent_y // 2, 2)
    center_fine, east_fine, west_fine, north_fine, south_fine = (grouped[0], grouped[1], grouped[2], grouped[3], grouped[4])
    center = center_fine.sum(axis=(1, 3)) + east_fine[:, 0].sum(axis=2) + west_fine[:, 1].sum(axis=2) + north_fine[:, :, :, 0].sum(axis=1) + south_fine[:, :, :, 1].sum(axis=1)
    east_link = east_fine[:, 1].sum(axis=2)
    west_link = west_fine[:, 0].sum(axis=2)
    north_link = north_fine[:, :, :, 1].sum(axis=1)
    south_link = south_fine[:, :, :, 0].sum(axis=1)
    return jnp.stack([center, east_link, west_link, north_link, south_link])

def restrict(values):
    extent_x, extent_y = values.shape
    return values.reshape(extent_x // 2, 2, extent_y // 2, 2).sum(axis=(1, 3))

def prolong(values):
    return jnp.repeat(jnp.repeat(values, 2, axis=0), 2, axis=1)

def vcycle(source, hierarchy, padder, coarse_solve):
    if len(hierarchy) == 1:
        return coarse_solve(source, hierarchy[0])
    coeffs = hierarchy[0]
    iterate = relax_factor * source / coeffs[0]
    residue = source - level_apply(iterate, coeffs, padder)
    correction = vcycle(restrict(residue), hierarchy[1:], padder, coarse_solve)
    iterate = iterate + prolong(correction)
    return jacobi_sweep(iterate, source, coeffs, padder)

def block_inverse(matrix):
    extent = matrix.shape[0]
    identity = jnp.eye(extent, dtype=matrix.dtype)[:, :, None, None] * jnp.ones_like(matrix[0, 0])
    left_part, right_part = (matrix, identity)
    for pivot_row in range(extent):
        pivot_value = left_part[pivot_row, pivot_row]
        scaled_left = left_part[pivot_row] / pivot_value
        scaled_right = right_part[pivot_row] / pivot_value
        factor = left_part[:, pivot_row]
        left_part = left_part - factor[:, None] * scaled_left[None]
        right_part = right_part - factor[:, None] * scaled_right[None]
        left_part = left_part.at[pivot_row].set(scaled_left)
        right_part = right_part.at[pivot_row].set(scaled_right)
    return right_part

def pressure_coeffs(eff_diag, weights, face_trans, ghosts):

    def weighed(side_values):
        return lax.optimization_barrier(jnp.sum(weights * side_values, axis=0))
    center = lax.optimization_barrier(jnp.sum(weights * eff_diag[:, 0], axis=0))
    return jnp.stack([center, -face_trans[0] * weighed(ghosts[0]), -face_trans[1] * weighed(ghosts[1]), -face_trans[2] * weighed(ghosts[2]), -face_trans[3] * weighed(ghosts[3])])

def least_squares(start_norm, columns):
    steps_count = len(columns)
    rhs_list = [start_norm] + [jnp.zeros_like(start_norm)] * steps_count
    cosine_values, sine_values, upper_columns = ([], [], [])
    for column_no in range(steps_count):
        column = list(columns[column_no])
        for earlier in range(column_no):
            first_entry = column[earlier]
            second_entry = column[earlier + 1]
            column[earlier] = cosine_values[earlier] * first_entry + sine_values[earlier] * second_entry
            column[earlier + 1] = -sine_values[earlier] * first_entry + cosine_values[earlier] * second_entry
        radius = jnp.sqrt(column[column_no] * column[column_no] + column[column_no + 1] * column[column_no + 1])
        cosine_value = column[column_no] / radius
        sine_value = column[column_no + 1] / radius
        column[column_no] = radius
        rhs_list[column_no + 1] = -sine_value * rhs_list[column_no]
        rhs_list[column_no] = cosine_value * rhs_list[column_no]
        cosine_values.append(cosine_value)
        sine_values.append(sine_value)
        upper_columns.append(column)
    coefficients = [None] * steps_count
    for row_no in reversed(range(steps_count)):
        running = rhs_list[row_no]
        for later_no in range(row_no + 1, steps_count):
            running = running - upper_columns[later_no][row_no] * coefficients[later_no]
        coefficients[row_no] = running / upper_columns[row_no][row_no]
    return (coefficients, jnp.abs(rhs_list[steps_count]))

def reference(right_side, diag_blocks, couple_blocks, transmissibility, pressure_weights, well_mask):
    identity = jnp.eye(NC, dtype=diag_blocks.dtype)[:, :, None, None]
    eff_diag = diag_blocks + well_boost * well_mask.astype(diag_blocks.dtype)[None, None] * identity
    inverse = block_inverse(eff_diag)
    ghosts = four_sides(pad_cells(couple_blocks[:, 0]))
    hierarchy = [pressure_coeffs(eff_diag, pressure_weights, transmissibility, ghosts)]
    for level_no in range(LEVELS - 1):
        hierarchy.append(coarsen(hierarchy[-1]))

    def coarse_solve(source, coeffs):
        return coarse_sweeps(source, coeffs, pad_cells)

    def apply_full(vector):
        return apply_blocks(vector, eff_diag, couple_blocks, transmissibility, pad_cells)

    def precondition(vector):
        pressure_rhs = lax.optimization_barrier(jnp.sum(pressure_weights * vector, axis=0))
        pressure = vcycle(pressure_rhs, hierarchy, pad_cells, coarse_solve)
        lifted = jnp.concatenate([pressure[None], jnp.zeros((NC - 1,) + pressure.shape, pressure.dtype)])
        second = vector - apply_full(lifted)
        return lifted + lax.optimization_barrier(jnp.sum(inverse * second[None], axis=1))
    start_norm = jnp.sqrt(jnp.sum(right_side * right_side))
    krylov_basis = [right_side / start_norm]
    directions, columns = ([], [])
    for step_no in range(GSTEPS):
        direction = precondition(krylov_basis[step_no])
        directions.append(direction)
        mapped = apply_full(direction)
        projections = [jnp.sum(mapped * member) for member in krylov_basis]
        remainder = mapped
        for projection, member in zip(projections, krylov_basis):
            remainder = remainder - projection * member
        length = jnp.sqrt(jnp.sum(remainder * remainder))
        krylov_basis.append(remainder / length)
        columns.append(projections + [length])
    coefficients, estimate = least_squares(start_norm, columns)
    solution = coefficients[0] * directions[0]
    for step_no in range(1, GSTEPS):
        solution = solution + coefficients[step_no] * directions[step_no]
    return (solution, estimate)
```

```python
import functools

import jax
import jax.numpy as jnp
from jax import lax
from jax.experimental import pallas as pl
from jax.experimental.pallas import tpu as pltpu
from jax.sharding import PartitionSpec as P

COARSE_SWEEPS = 6
RELAX = 0.8
KEEP = 1.0 - RELAX
BOOST = 8.0
MESH = pl.DeviceIdType.MESH
PIECE = 32
SIDES = ((-1, 0), (1, 0), (0, -1), (0, 1))
CORNERS = ((-1, -1), (-1, 1), (1, -1), (1, 1))


def roll(x, shift, axis):
    shift = shift % x.shape[axis]
    return x if shift == 0 else pltpu.roll(x, shift, axis)


def kernel(gx, gy, b_hbm, diag_hbm, couple_hbm, trans_hbm, weights_hbm, well_hbm, out_hbm, est_ref,
           vb, vd, vc, vt, vw, vwell, inv, coup, prod, z1, w1, q1, srow, rrow, scol, rcol,
           sown, spack, rx, ry, rd, sf, rfx, rfy, rfd, ext, link0, scaled0, link1, scaled1,
           scaled2, recip, fext, vout, sred, redy, sredx, redx,
           in_sem, ssem, rsem, ysend, yrecv, xsend, xrecv):
    nc, rows, cols = vb.shape
    ix, iy = lax.axis_index("gx"), lax.axis_index("gy")
    has = {(-1, 0): ix > 0, (1, 0): ix < gx - 1, (0, -1): iy > 0, (0, 1): iy < gy - 1}
    for dx, dy in CORNERS:
        has[(dx, dy)] = jnp.logical_and(has[(dx, 0)], has[(0, dy)])

    loads = []
    for n, (src, dst) in enumerate((
        (couple_hbm.at[:, 0], vc.at[:, 0]),
        (weights_hbm, vw),
        (trans_hbm, vt),
        (b_hbm, vb),
        (well_hbm, vwell),
        (diag_hbm, vd),
        (couple_hbm.at[:, pl.ds(1, nc - 1)], vc.at[:, pl.ds(1, nc - 1)]),
    )):
        copy = pltpu.make_async_copy(src, dst, in_sem.at[n])
        copy.start()
        loads.append(copy)

    row = lax.broadcasted_iota(jnp.int32, (rows, cols), 0)
    lane = lax.broadcasted_iota(jnp.int32, (rows, cols), 1)
    zero = jnp.zeros((rows, cols), jnp.float32)
    ones = jnp.ones((rows, cols), jnp.float32)

    first_piece = jnp.where(lane < PIECE, 1.0, 0.0)
    for s in range(2):
        for i in range(6):
            rx[s, i] = ones if i == 0 else zero
        ry[s, 0] = first_piece
        ry[s, 1] = zero
        rfx[s] = zero
        rfy[s] = zero
        for r in range(3):
            rrow[r, s] = jnp.zeros(rrow.shape[2:], jnp.float32)
            rcol[r, s] = zero
    for s in range(4):
        rd[s, 0] = first_piece
        rd[s, 1] = zero
        rfd[s] = zero

    barrier = pltpu.get_barrier_semaphore()
    for d in range(1, gy):
        pl.semaphore_signal(barrier, inc=1, device_id=(ix, lax.rem(iy + d, gy)), device_id_type=MESH)
    for d in range(1, gx):
        pl.semaphore_signal(barrier, inc=1, device_id=(lax.rem(ix + d, gx), iy), device_id_type=MESH)
    for dx, dy in CORNERS:
        @pl.when(has[(dx, dy)])
        def _(dx=dx, dy=dy):
            pl.semaphore_signal(barrier, inc=1, device_id=(ix + dx, iy + dy), device_id_type=MESH)
    near_x = has[(-1, 0)].astype(jnp.int32) + has[(1, 0)].astype(jnp.int32)
    near_y = has[(0, -1)].astype(jnp.int32) + has[(0, 1)].astype(jnp.int32)
    pl.semaphore_wait(barrier, gx + gy - 2 + near_x * near_y)

    sent = []

    def describe(k, src, dst, dx, dy):
        return pltpu.make_async_remote_copy(
            src_ref=src, dst_ref=dst, send_sem=ssem.at[k], recv_sem=rsem.at[k],
            device_id=(ix + dx, iy + dy), device_id_type=MESH)

    def send(k, src, dst, dx, dy):
        @pl.when(has[(dx, dy)])
        def _():
            describe(k, src, dst, dx, dy).start()
        sent.append((k, src, dst, dx, dy))

    def receive(group):
        for k, src, dst, dx, dy in group:
            @pl.when(has[(-dx, -dy)])
            def _(k=k, src=src, dst=dst, dx=dx, dy=dy):
                describe(k, src, dst, dx, dy).wait_recv()

    def send_edges(r, plane):
        low, high = zero, zero
        for c in range(nc):
            value = plane(c)
            srow[r, 0, c:c + 1] = value[0:1]
            srow[r, 1, c:c + 1] = value[rows - 1:rows]
            low = jnp.where(lane == c, roll(value, c, 1), low)
            high = jnp.where(lane == c, roll(value, c + 1, 1), high)
        scol[r, 0] = low
        scol[r, 1] = high
        mark = len(sent)
        send(4 * r, srow.at[r, 0], rrow.at[r, 1], -1, 0)
        send(4 * r + 1, srow.at[r, 1], rrow.at[r, 0], 1, 0)
        send(4 * r + 2, scol.at[r, 0], rcol.at[r, 1], 0, -1)
        send(4 * r + 3, scol.at[r, 1], rcol.at[r, 0], 0, 1)
        return sent[mark:]

    def neighbours(r, c, value):
        up = jnp.where(row == rows - 1, rrow[r, 1, c:c + 1], roll(value, -1, 0))
        down = jnp.where(row == 0, rrow[r, 0, c:c + 1], roll(value, 1, 0))
        north = jnp.where(lane == cols - 1, roll(rcol[r, 1], cols - 1 - c, 1), roll(value, -1, 1))
        south = jnp.where(lane == 0, roll(rcol[r, 0], -c, 1), roll(value, 1, 1))
        return up, down, north, south

    loads[0].wait()
    group = send_edges(0, lambda c: vc[c, 0])
    for copy in loads[1:6]:
        copy.wait()
    boost = BOOST * vwell[...].astype(jnp.float32)
    for c in range(nc):
        vd[c, c] = vd[c, c] + boost
    center = zero
    rhs = zero
    for c in range(nc):
        center = center + vw[c] * vd[c, 0]
        rhs = rhs + vw[c] * vb[c]
    sown[0] = center
    sown[5] = rhs
    receive(group)
    links = [zero] * 4
    for c in range(nc):
        for d, value in enumerate(neighbours(0, c, vc[c, 0])):
            value = vt[d] * value
            coup[d, c] = value
            links[d] = links[d] - vw[c] * value
    for d in range(4):
        sown[1 + d] = links[d]

    for side in range(2):
        for t in range(2):
            tile = zero
            for j in range(4):
                i = 4 * t + j
                if i < 6:
                    shift = PIECE * j + (PIECE if side else 0)
                    inside = jnp.logical_and(lane >= PIECE * j, lane < PIECE * (j + 1))
                    tile = jnp.where(inside, roll(sown[i], shift, 1), tile)
            spack[side, t] = tile
    mark = len(sent)
    for n, (dx, dy) in enumerate(SIDES):
        if dx:
            send(12 + n, sown, rx.at[(1 - dx) // 2], dx, dy)
        else:
            send(12 + n, spack.at[(1 + dy) // 2], ry.at[(1 - dy) // 2], dx, dy)
    for n, (dx, dy) in enumerate(CORNERS):
        send(16 + n, spack.at[(1 + dy) // 2], rd.at[3 - n], dx, dy)
    group = sent[mark:]

    def invert(step, carry):
        at = pl.ds(pl.multiple_of(step * 8, 8), 8)
        for i in range(nc):
            for j in range(nc):
                inv[i, j, at] = vd[i, j, at]
        for p in range(nc):
            reciprocal = 1.0 / inv[p, p, at]
            scaled = [reciprocal if j == p else inv[p, j, at] * reciprocal for j in range(nc)]
            for j in range(nc):
                inv[p, j, at] = scaled[j]
            for i in range(nc):
                if i != p:
                    factor = inv[i, p, at]
                    for j in range(nc):
                        if j == p:
                            inv[i, j, at] = -factor * scaled[j]
                        else:
                            inv[i, j, at] = inv[i, j, at] - factor * scaled[j]
        return carry

    lax.fori_loop(0, rows // 8, invert, 0)
    receive(group)

    for i in range(6):
        t, j = i // 4, i % 4
        fill = ones if i == 0 else zero
        for block in range(3):
            own = (rx[0, i], sown[i], rx[1, i])[block]
            left = (rd[0, t], ry[0, t], rd[2, t])[block]
            right = (rd[1, t], ry[1, t], rd[3, t])[block]
            right = roll(right, -PIECE * j, 1)
            left = roll(left, cols - PIECE - PIECE * j, 1)
            halo = jnp.where(lane < PIECE, right, jnp.where(lane >= cols - PIECE, left, fill))
            target = fext if i == 5 else ext.at[i]
            target[block * rows:(block + 1) * rows, 0:cols] = own
            target[block * rows:(block + 1) * rows, cols:2 * cols] = halo

    wide = (3 * rows, 2 * cols)
    wrow = lax.broadcasted_iota(jnp.int32, wide, 0)
    wlane = lax.broadcasted_iota(jnp.int32, wide, 1)

    def aggregate(x, s):
        x = x + jnp.where((wrow & s) == 0, roll(x, -s, 0), roll(x, s, 0))
        return x + jnp.where((wlane & s) == 0, roll(x, -s, 1), roll(x, s, 1))

    def around(x, s):
        return roll(x, -s, 0), roll(x, s, 0), roll(x, -s, 1), roll(x, s, 1)

    level = [ext[i] for i in range(5)]
    for k in range(3):
        ratio = RELAX / level[0]
        recip[k] = ratio
        for d in range(4):
            (scaled0, scaled1, scaled2)[k][d] = ratio * level[1 + d]
            if k < 2:
                (link0, link1)[k][d] = level[1 + d]
        if k < 2:
            s = 1 << k
            even_x, even_y = (wrow & s) == 0, (wlane & s) == 0
            c0, east, west, north, south = level
            level = [
                aggregate(c0 + jnp.where(even_x, east, west) + jnp.where(even_y, north, south), s),
                aggregate(jnp.where(even_x, 0.0, east), s),
                aggregate(jnp.where(even_x, west, 0.0), s),
                aggregate(jnp.where(even_y, 0.0, north), s),
                aggregate(jnp.where(even_y, south, 0.0), s),
            ]

    def gather_links(coeffs, x, s):
        total = None
        for d, value in enumerate(around(x, s)):
            term = coeffs[d] * value
            total = term if total is None else total + term
        return total

    def vcycle():
        f0 = fext[...]
        g0 = recip[0] * f0
        f1 = aggregate(KEEP * f0 - gather_links(link0, g0, 1), 1)
        g1 = recip[1] * f1
        f2 = aggregate(KEEP * f1 - gather_links(link1, g1, 2), 2)
        g2 = recip[2] * f2
        e2 = g2
        for _ in range(COARSE_SWEEPS - 1):
            e2 = KEEP * e2 + g2 - gather_links(scaled2, e2, 4)
        e1 = g1 + e2
        e1 = KEEP * e1 + g1 - gather_links(scaled1, e1, 2)
        e0 = g0 + e1
        fext[...] = KEEP * e0 + g0 - gather_links(scaled0, e0, 1)
        e0 = fext[...]
        return tuple(x[rows:2 * rows, 0:cols] for x in (e0,) + around(e0, 1))

    def precondition(source, target):
        p = vcycle()
        for c in range(nc):
            total = source[c] - vd[c, 0] * p[0]
            for d in range(4):
                total = total + coup[d, c] * p[1 + d]
            prod[c] = total
        for c in range(nc):
            total = p[0] if c == 0 else zero
            for k in range(nc):
                total = total + inv[c, k] * prod[k]
            target[c] = total

    def operate(r, source, target):
        for c in range(nc):
            total = vc[c, 0] * source[0]
            for k in range(1, nc):
                total = total + vc[c, k] * source[k]
            prod[c] = total
        group = send_edges(r, lambda c: prod[c])
        for c in range(nc):
            total = vd[c, 0] * source[0]
            for k in range(1, nc):
                total = total + vd[c, k] * source[k]
            target[c] = total
        receive(group)
        for c in range(nc):
            total = target[c]
            for d, value in enumerate(neighbours(r, c, prod[c])):
                total = total - vt[d] * value
            target[c] = total

    def dot(x, y):
        total = zero
        for c in range(nc):
            total = total + x(c) * y(c)
        return jnp.sum(total, axis=0, keepdims=True)

    def reduce_y(n, parts):
        sred[n] = jnp.zeros(sred.shape[1:], jnp.float32)
        for i, part in enumerate(parts):
            sred[n, i:i + 1] = part
        copies = []
        for d in range(1, gy):
            copy = pltpu.make_async_remote_copy(
                src_ref=sred.at[n], dst_ref=redy.at[n, iy], send_sem=ysend.at[n, d - 1],
                recv_sem=yrecv.at[n, d - 1], device_id=(ix, lax.rem(iy + d, gy)), device_id_type=MESH)
            copy.start()
            copies.append(copy)
        redy[n, iy] = sred[n]
        return copies

    def reduce_x(n, copies):
        for copy in copies:
            copy.wait()
        total = redy[n, 0]
        for i in range(1, gy):
            total = total + redy[n, i]
        sredx[n] = total
        copies = []
        for d in range(1, gx):
            copy = pltpu.make_async_remote_copy(
                src_ref=sredx.at[n], dst_ref=redx.at[n, ix], send_sem=xsend.at[n, d - 1],
                recv_sem=xrecv.at[n, d - 1], device_id=(lax.rem(ix + d, gx), iy), device_id_type=MESH)
            copy.start()
            copies.append(copy)
        redx[n, ix] = total
        return copies

    def reduced(n, copies):
        for copy in copies:
            copy.wait()
        total = redx[n, 0]
        for i in range(1, gx):
            total = total + redx[n, i]
        total = jnp.sum(total, axis=1, keepdims=True)
        return total[0:1], total[1:2], total[2:3]

    precondition(vb, z1)
    loads[6].wait()
    operate(1, z1, w1)

    rhs = zero
    for c in range(nc):
        rhs = rhs + vw[c] * w1[c]
    sf[...] = rhs
    mark = len(sent)
    for n, (dx, dy) in enumerate(SIDES):
        send(20 + n, sf, (rfx.at[(1 - dx) // 2] if dx else rfy.at[(1 - dy) // 2]), dx, dy)
    for n, (dx, dy) in enumerate(CORNERS):
        send(24 + n, sf, rfd.at[3 - n], dx, dy)
    group = sent[mark:]
    copies = reduce_y(0, [
        dot(lambda c: vb[c], lambda c: vb[c]),
        dot(lambda c: vb[c], lambda c: w1[c]),
        dot(lambda c: w1[c], lambda c: w1[c]),
    ])
    receive(group)
    for block in range(3):
        own = (rfx[0], sf[...], rfx[1])[block]
        left = (rfd[0], rfy[0], rfd[2])[block]
        right = (rfd[1], rfy[1], rfd[3])[block]
        fext[block * rows:(block + 1) * rows, 0:cols] = own
        fext[block * rows:(block + 1) * rows, cols:2 * cols] = jnp.where(lane < cols // 2, right, left)
    precondition(w1, q1)
    copies = reduce_x(0, copies)
    operate(2, q1, vout)

    bb, bw, ww = reduced(0, copies)
    beta = jnp.sqrt(bb)
    h11 = bw / bb
    h21 = jnp.sqrt(ww / bb - h11 * h11)
    scale = 1.0 / (beta * h21)
    over = 1.0 / beta

    def mapped(c):
        return (vout[c] - h11 * w1[c]) * scale

    def basis2(c):
        return (w1[c] - h11 * vb[c]) * scale

    copies = reduce_y(1, [
        dot(mapped, lambda c: vb[c] * over),
        dot(mapped, basis2),
        dot(mapped, mapped),
    ])
    h12, h22, squared = reduced(1, reduce_x(1, copies))
    h32 = jnp.sqrt(squared - h12 * h12 - h22 * h22)

    radius1 = jnp.sqrt(h11 * h11 + h21 * h21)
    cos1, sin1 = h11 / radius1, h21 / radius1
    top, low = cos1 * h12 + sin1 * h22, -sin1 * h12 + cos1 * h22
    radius2 = jnp.sqrt(low * low + h32 * h32)
    cos2, sin2 = low / radius2, h32 / radius2
    g0, g1 = cos1 * beta, -sin1 * beta
    g1, g2 = cos2 * g1, -sin2 * g1
    y2 = g1 / radius2
    y1 = (g0 - top * y2) / radius1
    est_ref[...] = jnp.abs(g2)
    second = y2 * scale
    first = y1 * over - second * h11
    for c in range(nc):
        out_hbm[c] = first * z1[c] + second * q1[c]

    for k, src, dst, dx, dy in sent:
        @pl.when(has[(dx, dy)])
        def _(k=k, src=src, dst=dst, dx=dx, dy=dy):
            describe(k, src, dst, dx, dy).wait_send()


def on_device(gx, gy, right_side, diag, couple, trans, weights, well):
    nc, rows, cols = right_side.shape
    f32 = jnp.float32
    wide = (3 * rows, 2 * cols)
    vm = lambda *shape: pltpu.VMEM(shape, f32)
    dma = lambda *shape: pltpu.SemaphoreType.DMA(shape)
    field = (nc, rows, cols)
    pad = -(-nc // 8) * 8
    out, est = pl.pallas_call(
        functools.partial(kernel, gx, gy),
        name="cpr_gmres",
        out_shape=(jax.ShapeDtypeStruct(field, f32), jax.ShapeDtypeStruct((1, 1), f32)),
        in_specs=[pl.BlockSpec(memory_space=pl.ANY)] * 6,
        out_specs=(pl.BlockSpec(memory_space=pltpu.VMEM), pl.BlockSpec(memory_space=pltpu.VMEM)),
        scratch_shapes=[
            vm(*field), vm(nc, *field), vm(nc, *field), vm(4, rows, cols), vm(*field),
            pltpu.VMEM((rows, cols), jnp.int32), vm(nc, *field), vm(4, *field),
            vm(*field), vm(*field), vm(*field), vm(*field),
            vm(3, 2, pad, cols), vm(3, 2, pad, cols), vm(3, 2, rows, cols), vm(3, 2, rows, cols),
            vm(6, rows, cols), vm(2, 2, rows, cols), vm(2, 6, rows, cols), vm(2, 2, rows, cols),
            vm(4, 2, rows, cols), vm(rows, cols), vm(2, rows, cols), vm(2, rows, cols),
            vm(4, rows, cols),
            vm(5, *wide), vm(4, *wide), vm(4, *wide), vm(4, *wide), vm(4, *wide),
            vm(4, *wide), vm(3, *wide), vm(*wide), vm(*field),
            vm(2, 8, cols), vm(2, gy, 8, cols), vm(2, 8, cols), vm(2, gx, 8, cols),
            dma(7), dma(28), dma(28), dma(2, gy - 1), dma(2, gy - 1), dma(2, gx - 1), dma(2, gx - 1),
        ],
        compiler_params=pltpu.CompilerParams(
            collective_id=0, has_side_effects=True, vmem_limit_bytes=48 << 20),
    )(right_side, diag, couple, trans, weights, well)
    return out, est.reshape(())


def solution(mesh):
    return jax.shard_map(
        functools.partial(on_device, mesh.shape["gx"], mesh.shape["gy"]),
        mesh=mesh,
        in_specs=(
            P(None, "gx", "gy"),
            P(None, None, "gx", "gy"),
            P(None, None, "gx", "gy"),
            P(None, "gx", "gy"),
            P(None, "gx", "gy"),
            P("gx", "gy"),
        ),
        out_specs=(P(None, "gx", "gy"), P()),
        check_vma=False,
    )
```

```python
import functools

import jax
import jax.numpy as jnp
from jax import lax
from jax.experimental import pallas as pl
from jax.experimental.pallas import tpu as pltpu
from jax.sharding import PartitionSpec as P

COARSE_SWEEPS = 6
RELAX = 0.8
KEEP = 1.0 - RELAX
BOOST = 8.0
MESH = pl.DeviceIdType.MESH
PIECE = 32
SIDES = ((-1, 0), (1, 0), (0, -1), (0, 1))
CORNERS = ((-1, -1), (-1, 1), (1, -1), (1, 1))


def roll(x, shift, axis):
    shift = shift % x.shape[axis]
    return x if shift == 0 else pltpu.roll(x, shift, axis)


def kernel(gx, gy, b_hbm, diag_hbm, couple_hbm, trans_hbm, weights_hbm, well_hbm, out_hbm, est_ref,
           vb, vd, vc, vt, vw, vwell, inv, coup, prod, z1, w1, q1, srow, rrow, scol, rcol,
           sown, spack, rx, ry, rd, sf, rfx, rfy, rfd, ext, link0, scaled0, link1, scaled1,
           scaled2, recip, fext, vout, sred, redy, sredx, redx,
           in_sem, ssem, rsem, ysend, yrecv, xsend, xrecv):
    nc, rows, cols = vb.shape
    ix, iy = lax.axis_index("gx"), lax.axis_index("gy")
    has = {(-1, 0): ix > 0, (1, 0): ix < gx - 1, (0, -1): iy > 0, (0, 1): iy < gy - 1}
    for dx, dy in CORNERS:
        has[(dx, dy)] = jnp.logical_and(has[(dx, 0)], has[(0, dy)])

    loads = []
    for n, (src, dst) in enumerate((
        (couple_hbm.at[:, 0], vc.at[:, 0]),
        (weights_hbm, vw),
        (trans_hbm, vt),
        (b_hbm, vb),
        (well_hbm, vwell),
        (diag_hbm, vd),
        (couple_hbm.at[:, pl.ds(1, nc - 1)], vc.at[:, pl.ds(1, nc - 1)]),
    )):
        copy = pltpu.make_async_copy(src, dst, in_sem.at[n])
        copy.start()
        loads.append(copy)

    row = lax.broadcasted_iota(jnp.int32, (rows, cols), 0)
    lane = lax.broadcasted_iota(jnp.int32, (rows, cols), 1)
    zero = jnp.zeros((rows, cols), jnp.float32)
    ones = jnp.ones((rows, cols), jnp.float32)

    first_piece = jnp.where(lane < PIECE, 1.0, 0.0)
    for s in range(2):
        for i in range(6):
            rx[s, i] = ones if i == 0 else zero
        ry[s, 0] = first_piece
        ry[s, 1] = zero
        rfx[s] = zero
        rfy[s] = zero
        for r in range(3):
            rrow[r, s] = jnp.zeros(rrow.shape[2:], jnp.float32)
            rcol[r, s] = zero
    for s in range(4):
        rd[s, 0] = first_piece
        rd[s, 1] = zero
        rfd[s] = zero

    barrier = pltpu.get_barrier_semaphore()
    for d in range(1, gy):
        pl.semaphore_signal(barrier, inc=1, device_id=(ix, lax.rem(iy + d, gy)), device_id_type=MESH)
    for d in range(1, gx):
        pl.semaphore_signal(barrier, inc=1, device_id=(lax.rem(ix + d, gx), iy), device_id_type=MESH)
    for dx, dy in CORNERS:
        @pl.when(has[(dx, dy)])
        def _(dx=dx, dy=dy):
            pl.semaphore_signal(barrier, inc=1, device_id=(ix + dx, iy + dy), device_id_type=MESH)
    near_x = has[(-1, 0)].astype(jnp.int32) + has[(1, 0)].astype(jnp.int32)
    near_y = has[(0, -1)].astype(jnp.int32) + has[(0, 1)].astype(jnp.int32)
    pl.semaphore_wait(barrier, gx + gy - 2 + near_x * near_y)

    sent = []

    def describe(k, src, dst, dx, dy):
        return pltpu.make_async_remote_copy(
            src_ref=src, dst_ref=dst, send_sem=ssem.at[k], recv_sem=rsem.at[k],
            device_id=(ix + dx, iy + dy), device_id_type=MESH)

    def send(k, src, dst, dx, dy):
        @pl.when(has[(dx, dy)])
        def _():
            describe(k, src, dst, dx, dy).start()
        sent.append((k, src, dst, dx, dy))

    def receive(group):
        for k, src, dst, dx, dy in group:
            @pl.when(has[(-dx, -dy)])
            def _(k=k, src=src, dst=dst, dx=dx, dy=dy):
                describe(k, src, dst, dx, dy).wait_recv()

    def send_edges(r, plane):
        low, high = zero, zero
        for c in range(nc):
            value = plane(c)
            srow[r, 0, c:c + 1] = value[0:1]
            srow[r, 1, c:c + 1] = value[rows - 1:rows]
            low = jnp.where(lane == c, roll(value, c, 1), low)
            high = jnp.where(lane == c, roll(value, c + 1, 1), high)
        scol[r, 0] = low
        scol[r, 1] = high
        mark = len(sent)
        send(4 * r, srow.at[r, 0], rrow.at[r, 1], -1, 0)
        send(4 * r + 1, srow.at[r, 1], rrow.at[r, 0], 1, 0)
        send(4 * r + 2, scol.at[r, 0], rcol.at[r, 1], 0, -1)
        send(4 * r + 3, scol.at[r, 1], rcol.at[r, 0], 0, 1)
        return sent[mark:]

    def neighbours(r, c, value):
        up = jnp.where(row == rows - 1, rrow[r, 1, c:c + 1], roll(value, -1, 0))
        down = jnp.where(row == 0, rrow[r, 0, c:c + 1], roll(value, 1, 0))
        north = jnp.where(lane == cols - 1, roll(rcol[r, 1], cols - 1 - c, 1), roll(value, -1, 1))
        south = jnp.where(lane == 0, roll(rcol[r, 0], -c, 1), roll(value, 1, 1))
        return up, down, north, south

    loads[0].wait()
    group = send_edges(0, lambda c: vc[c, 0])
    for copy in loads[1:6]:
        copy.wait()
    boost = BOOST * vwell[...].astype(jnp.float32)
    for c in range(nc):
        vd[c, c] = vd[c, c] + boost
    center = zero
    rhs = zero
    for c in range(nc):
        center = center + vw[c] * vd[c, 0]
        rhs = rhs + vw[c] * vb[c]
    sown[0] = center
    sown[5] = rhs
    receive(group)
    links = [zero] * 4
    for c in range(nc):
        for d, value in enumerate(neighbours(0, c, vc[c, 0])):
            value = vt[d] * value
            coup[d, c] = value
            links[d] = links[d] - vw[c] * value
    for d in range(4):
        sown[1 + d] = links[d]

    for side in range(2):
        for t in range(2):
            tile = zero
            for j in range(4):
                i = 4 * t + j
                if i < 6:
                    shift = PIECE * j + (PIECE if side else 0)
                    inside = jnp.logical_and(lane >= PIECE * j, lane < PIECE * (j + 1))
                    tile = jnp.where(inside, roll(sown[i], shift, 1), tile)
            spack[side, t] = tile
    mark = len(sent)
    for n, (dx, dy) in enumerate(SIDES):
        if dx:
            send(12 + n, sown, rx.at[(1 - dx) // 2], dx, dy)
        else:
            send(12 + n, spack.at[(1 + dy) // 2], ry.at[(1 - dy) // 2], dx, dy)
    for n, (dx, dy) in enumerate(CORNERS):
        send(16 + n, spack.at[(1 + dy) // 2], rd.at[3 - n], dx, dy)
    group = sent[mark:]

    def invert(step, carry):
        at = pl.ds(pl.multiple_of(step * 8, 8), 8)
        for i in range(nc):
            for j in range(nc):
                inv[i, j, at] = vd[i, j, at]
        for p in range(nc):
            reciprocal = 1.0 / inv[p, p, at]
            scaled = [reciprocal if j == p else inv[p, j, at] * reciprocal for j in range(nc)]
            for j in range(nc):
                inv[p, j, at] = scaled[j]
            for i in range(nc):
                if i != p:
                    factor = inv[i, p, at]
                    for j in range(nc):
                        if j == p:
                            inv[i, j, at] = -factor * scaled[j]
                        else:
                            inv[i, j, at] = inv[i, j, at] - factor * scaled[j]
        return carry

    lax.fori_loop(0, rows // 8, invert, 0)
    receive(group)

    for i in range(6):
        t, j = i // 4, i % 4
        fill = ones if i == 0 else zero
        for block in range(3):
            own = (rx[0, i], sown[i], rx[1, i])[block]
            left = (rd[0, t], ry[0, t], rd[2, t])[block]
            right = (rd[1, t], ry[1, t], rd[3, t])[block]
            right = roll(right, -PIECE * j, 1)
            left = roll(left, cols - PIECE - PIECE * j, 1)
            halo = jnp.where(lane < PIECE, right, jnp.where(lane >= cols - PIECE, left, fill))
            target = fext if i == 5 else ext.at[i]
            target[block * rows:(block + 1) * rows, 0:cols] = own
            target[block * rows:(block + 1) * rows, cols:2 * cols] = halo

    wide = (3 * rows, 2 * cols)
    wrow = lax.broadcasted_iota(jnp.int32, wide, 0)
    wlane = lax.broadcasted_iota(jnp.int32, wide, 1)

    def aggregate(x, s):
        x = x + jnp.where((wrow & s) == 0, roll(x, -s, 0), roll(x, s, 0))
        return x + jnp.where((wlane & s) == 0, roll(x, -s, 1), roll(x, s, 1))

    def around(x, s):
        return roll(x, -s, 0), roll(x, s, 0), roll(x, -s, 1), roll(x, s, 1)

    level = [ext[i] for i in range(5)]
    for k in range(3):
        ratio = RELAX / level[0]
        recip[k] = ratio
        for d in range(4):
            (scaled0, scaled1, scaled2)[k][d] = ratio * level[1 + d]
            if k < 2:
                (link0, link1)[k][d] = level[1 + d]
        if k < 2:
            s = 1 << k
            even_x, even_y = (wrow & s) == 0, (wlane & s) == 0
            c0, east, west, north, south = level
            level = [
                aggregate(c0 + jnp.where(even_x, east, west) + jnp.where(even_y, north, south), s),
                aggregate(jnp.where(even_x, 0.0, east), s),
                aggregate(jnp.where(even_x, west, 0.0), s),
                aggregate(jnp.where(even_y, 0.0, north), s),
                aggregate(jnp.where(even_y, south, 0.0), s),
            ]

    def gather_links(coeffs, x, s):
        total = None
        for d, value in enumerate(around(x, s)):
            term = coeffs[d] * value
            total = term if total is None else total + term
        return total

    def vcycle():
        f0 = fext[...]
        g0 = recip[0] * f0
        f1 = aggregate(KEEP * f0 - gather_links(link0, g0, 1), 1)
        g1 = recip[1] * f1
        f2 = aggregate(KEEP * f1 - gather_links(link1, g1, 2), 2)
        g2 = recip[2] * f2
        e2 = g2
        for _ in range(COARSE_SWEEPS - 1):
            e2 = KEEP * e2 + g2 - gather_links(scaled2, e2, 4)
        e1 = g1 + e2
        e1 = KEEP * e1 + g1 - gather_links(scaled1, e1, 2)
        e0 = g0 + e1
        fext[...] = KEEP * e0 + g0 - gather_links(scaled0, e0, 1)
        e0 = fext[...]
        return tuple(x[rows:2 * rows, 0:cols] for x in (e0,) + around(e0, 1))

    def precondition(source, target):
        p = vcycle()
        for c in range(nc):
            total = source[c] - vd[c, 0] * p[0]
            for d in range(4):
                total = total + coup[d, c] * p[1 + d]
            prod[c] = total
        for c in range(nc):
            total = p[0] if c == 0 else zero
            for k in range(nc):
                total = total + inv[c, k] * prod[k]
            target[c] = total

    def operate(r, source, target):
        for c in range(nc):
            total = vc[c, 0] * source[0]
            for k in range(1, nc):
                total = total + vc[c, k] * source[k]
            prod[c] = total
        group = send_edges(r, lambda c: prod[c])
        for c in range(nc):
            total = vd[c, 0] * source[0]
            for k in range(1, nc):
                total = total + vd[c, k] * source[k]
            target[c] = total
        receive(group)
        for c in range(nc):
            total = target[c]
            for d, value in enumerate(neighbours(r, c, prod[c])):
                total = total - vt[d] * value
            target[c] = total

    def dot(x, y):
        total = zero
        for c in range(nc):
            total = total + x(c) * y(c)
        return jnp.sum(total, axis=0, keepdims=True)

    def reduce_y(n, parts):
        sred[n] = jnp.zeros(sred.shape[1:], jnp.float32)
        for i, part in enumerate(parts):
            sred[n, i:i + 1] = part
        copies = []
        for d in range(1, gy):
            copy = pltpu.make_async_remote_copy(
                src_ref=sred.at[n], dst_ref=redy.at[n, iy], send_sem=ysend.at[n, d - 1],
                recv_sem=yrecv.at[n, d - 1], device_id=(ix, lax.rem(iy + d, gy)), device_id_type=MESH)
            copy.start()
            copies.append(copy)
        redy[n, iy] = sred[n]
        return copies

    def reduce_x(n, copies):
        for copy in copies:
            copy.wait()
        total = redy[n, 0]
        for i in range(1, gy):
            total = total + redy[n, i]
        sredx[n] = total
        copies = []
        for d in range(1, gx):
            copy = pltpu.make_async_remote_copy(
                src_ref=sredx.at[n], dst_ref=redx.at[n, ix], send_sem=xsend.at[n, d - 1],
                recv_sem=xrecv.at[n, d - 1], device_id=(lax.rem(ix + d, gx), iy), device_id_type=MESH)
            copy.start()
            copies.append(copy)
        redx[n, ix] = total
        return copies

    def reduced(n, copies):
        for copy in copies:
            copy.wait()
        total = redx[n, 0]
        for i in range(1, gx):
            total = total + redx[n, i]
        total = jnp.sum(total, axis=1, keepdims=True)
        return total[0:1], total[1:2], total[2:3]

    precondition(vb, z1)
    loads[6].wait()
    operate(1, z1, w1)

    rhs = zero
    for c in range(nc):
        rhs = rhs + vw[c] * w1[c]
    sf[...] = rhs
    mark = len(sent)
    for n, (dx, dy) in enumerate(SIDES):
        send(20 + n, sf, (rfx.at[(1 - dx) // 2] if dx else rfy.at[(1 - dy) // 2]), dx, dy)
    for n, (dx, dy) in enumerate(CORNERS):
        send(24 + n, sf, rfd.at[3 - n], dx, dy)
    group = sent[mark:]
    copies = reduce_y(0, [
        dot(lambda c: vb[c], lambda c: vb[c]),
        dot(lambda c: vb[c], lambda c: w1[c]),
        dot(lambda c: w1[c], lambda c: w1[c]),
    ])
    receive(group)
    for block in range(3):
        own = (rfx[0], sf[...], rfx[1])[block]
        left = (rfd[0], rfy[0], rfd[2])[block]
        right = (rfd[1], rfy[1], rfd[3])[block]
        fext[block * rows:(block + 1) * rows, 0:cols] = own
        fext[block * rows:(block + 1) * rows, cols:2 * cols] = jnp.where(lane < cols // 2, right, left)
    precondition(w1, q1)
    copies = reduce_x(0, copies)
    operate(2, q1, vout)

    bb, bw, ww = reduced(0, copies)
    beta = jnp.sqrt(bb)
    h11 = bw / bb
    h21 = jnp.sqrt(ww / bb - h11 * h11)
    scale = 1.0 / (beta * h21)
    over = 1.0 / beta

    def mapped(c):
        return (vout[c] - h11 * w1[c]) * scale

    def basis2(c):
        return (w1[c] - h11 * vb[c]) * scale

    copies = reduce_y(1, [
        dot(mapped, lambda c: vb[c] * over),
        dot(mapped, basis2),
        dot(mapped, mapped),
    ])
    h12, h22, squared = reduced(1, reduce_x(1, copies))
    h32 = jnp.sqrt(squared - h12 * h12 - h22 * h22)

    radius1 = jnp.sqrt(h11 * h11 + h21 * h21)
    cos1, sin1 = h11 / radius1, h21 / radius1
    top, low = cos1 * h12 + sin1 * h22, -sin1 * h12 + cos1 * h22
    radius2 = jnp.sqrt(low * low + h32 * h32)
    cos2, sin2 = low / radius2, h32 / radius2
    g0, g1 = cos1 * beta, -sin1 * beta
    g1, g2 = cos2 * g1, -sin2 * g1
    y2 = g1 / radius2
    y1 = (g0 - top * y2) / radius1
    est_ref[...] = jnp.abs(g2)
    second = y2 * scale
    first = y1 * over - second * h11
    for c in range(nc):
        out_hbm[c] = first * z1[c] + second * q1[c]

    for k, src, dst, dx, dy in sent:
        @pl.when(has[(dx, dy)])
        def _(k=k, src=src, dst=dst, dx=dx, dy=dy):
            describe(k, src, dst, dx, dy).wait_send()


def on_device(gx, gy, right_side, diag, couple, trans, weights, well):
    nc, rows, cols = right_side.shape
    f32 = jnp.float32
    wide = (3 * rows, 2 * cols)
    vm = lambda *shape: pltpu.VMEM(shape, f32)
    dma = lambda *shape: pltpu.SemaphoreType.DMA(shape)
    field = (nc, rows, cols)
    pad = -(-nc // 8) * 8
    out, est = pl.pallas_call(
        functools.partial(kernel, gx, gy),
        name="cpr_gmres",
        out_shape=(jax.ShapeDtypeStruct(field, f32), jax.ShapeDtypeStruct((1, 1), f32)),
        in_specs=[pl.BlockSpec(memory_space=pltpu.HBM)] * 6,
        out_specs=(pl.BlockSpec(memory_space=pltpu.VMEM), pl.BlockSpec(memory_space=pltpu.VMEM)),
        scratch_shapes=[
            vm(*field), vm(nc, *field), vm(nc, *field), vm(4, rows, cols), vm(*field),
            pltpu.VMEM((rows, cols), jnp.int32), vm(nc, *field), vm(4, *field),
            vm(*field), vm(*field), vm(*field), vm(*field),
            vm(3, 2, pad, cols), vm(3, 2, pad, cols), vm(3, 2, rows, cols), vm(3, 2, rows, cols),
            vm(6, rows, cols), vm(2, 2, rows, cols), vm(2, 6, rows, cols), vm(2, 2, rows, cols),
            vm(4, 2, rows, cols), vm(rows, cols), vm(2, rows, cols), vm(2, rows, cols),
            vm(4, rows, cols),
            vm(5, *wide), vm(4, *wide), vm(4, *wide), vm(4, *wide), vm(4, *wide),
            vm(4, *wide), vm(3, *wide), vm(*wide), vm(*field),
            vm(2, 8, cols), vm(2, gy, 8, cols), vm(2, 8, cols), vm(2, gx, 8, cols),
            dma(7), dma(28), dma(28), dma(2, gy - 1), dma(2, gy - 1), dma(2, gx - 1), dma(2, gx - 1),
        ],
        compiler_params=pltpu.CompilerParams(
            collective_id=0, has_side_effects=True, vmem_limit_bytes=60 << 20),
    )(right_side, diag, couple, trans, weights, well)
    return out, est.reshape(())


def solution(mesh):
    return jax.shard_map(
        functools.partial(on_device, mesh.shape["gx"], mesh.shape["gy"]),
        mesh=mesh,
        in_specs=(
            P(None, "gx", "gy"),
            P(None, None, "gx", "gy"),
            P(None, None, "gx", "gy"),
            P(None, "gx", "gy"),
            P(None, "gx", "gy"),
            P("gx", "gy"),
        ),
        out_specs=(P(None, "gx", "gy"), P()),
        check_vma=False,
    )
```

```python
import functools

import jax
import jax.numpy as jnp
from jax import lax
from jax.experimental import pallas as pl
from jax.experimental.pallas import tpu as pltpu
from jax.sharding import PartitionSpec as P

COARSE_SWEEPS = 6
RELAX = 0.8
KEEP = 1.0 - RELAX
BOOST = 8.0
MESH = pl.DeviceIdType.MESH
PIECE = 32
SIDES = ((-1, 0), (1, 0), (0, -1), (0, 1))
CORNERS = ((-1, -1), (-1, 1), (1, -1), (1, 1))


def roll(x, shift, axis):
    shift = shift % x.shape[axis]
    return x if shift == 0 else pltpu.roll(x, shift, axis)


def kernel(gx, gy, b_hbm, diag_hbm, couple_hbm, trans_hbm, weights_hbm, well_hbm, out_hbm, est_ref,
           vb, vd, vc, vt, vw, vwell, inv, coup, prod, z1, w1, q1, srow, rrow, scol, rcol,
           sown, spack, rx, ry, rd, sf, sfp, rfx, rfy, rfd, ext, link0, scaled0, link1, scaled1,
           scaled2, recip, fext, vout, sred, redall,
           in_sem, ssem, rsem, rsend, rrecv):
    nc, rows, cols = vb.shape
    ix, iy = lax.axis_index("gx"), lax.axis_index("gy")
    has = {(-1, 0): ix > 0, (1, 0): ix < gx - 1, (0, -1): iy > 0, (0, 1): iy < gy - 1}
    for dx, dy in CORNERS:
        has[(dx, dy)] = jnp.logical_and(has[(dx, 0)], has[(0, dy)])

    loads = []
    for n, (src, dst) in enumerate((
        (couple_hbm.at[:, 0], vc.at[:, 0]),
        (weights_hbm, vw),
        (trans_hbm, vt),
        (b_hbm, vb),
        (well_hbm, vwell),
        (diag_hbm.at[:, 0], vd.at[:, 0]),
        (diag_hbm.at[:, pl.ds(1, nc - 1)], vd.at[:, pl.ds(1, nc - 1)]),
        (couple_hbm.at[:, pl.ds(1, nc - 1)], vc.at[:, pl.ds(1, nc - 1)]),
    )):
        copy = pltpu.make_async_copy(src, dst, in_sem.at[n])
        copy.start()
        loads.append(copy)

    row = lax.broadcasted_iota(jnp.int32, (rows, cols), 0)
    lane = lax.broadcasted_iota(jnp.int32, (rows, cols), 1)
    zero = jnp.zeros((rows, cols), jnp.float32)
    ones = jnp.ones((rows, cols), jnp.float32)

    blank = jnp.zeros((8, cols), jnp.float32)
    for s in range(2):
        for i in range(6):
            rx[s, i] = ones if i == 0 else zero
            ry[s, i] = blank + 1.0 if i == 0 else blank
        rfx[s] = zero
        rfy[s] = blank
        for r in range(3):
            rrow[r, s] = jnp.zeros(rrow.shape[2:], jnp.float32)
            rcol[r, s] = zero
    for s in range(4):
        for i in range(6):
            rd[s, i] = blank + 1.0 if i == 0 else blank
        rfd[s] = blank

    barrier = pltpu.get_barrier_semaphore()
    count = gx * gy
    me = ix * gy + iy

    def greet(d, carry):
        target = lax.rem(me + d, count)
        pl.semaphore_signal(barrier, inc=1, device_id=(lax.div(target, gy), lax.rem(target, gy)),
                            device_id_type=MESH)
        return carry

    lax.fori_loop(1, count, greet, 0)
    pl.semaphore_wait(barrier, count - 1)

    groups = rows // 8
    tile_lane = lane[0:8]

    def pack(plane, side):
        tile = jnp.zeros((8, cols), jnp.float32)
        for j in range(groups):
            inside = jnp.logical_and(tile_lane >= PIECE * j, tile_lane < PIECE * (j + 1))
            tile = jnp.where(inside, roll(plane[8 * j:8 * j + 8], PIECE * (j + side), 1), tile)
        return tile

    def unpack(left, right, fill):
        parts = []
        for j in range(groups):
            first = roll(right, -PIECE * j, 1)
            last = roll(left, -PIECE * (j + 1), 1)
            parts.append(jnp.where(tile_lane < PIECE, first,
                                   jnp.where(tile_lane >= cols - PIECE, last, fill)))
        return jnp.concatenate(parts, axis=0)

    sent = []

    def describe(k, src, dst, dx, dy):
        return pltpu.make_async_remote_copy(
            src_ref=src, dst_ref=dst, send_sem=ssem.at[k], recv_sem=rsem.at[k],
            device_id=(ix + dx, iy + dy), device_id_type=MESH)

    def send(k, src, dst, dx, dy):
        @pl.when(has[(dx, dy)])
        def _():
            describe(k, src, dst, dx, dy).start()
        sent.append((k, src, dst, dx, dy))

    def receive(group):
        for k, src, dst, dx, dy in group:
            @pl.when(has[(-dx, -dy)])
            def _(k=k, src=src, dst=dst, dx=dx, dy=dy):
                describe(k, src, dst, dx, dy).wait_recv()

    def send_edges(r, plane):
        low, high = zero, zero
        for c in range(nc):
            value = plane(c)
            srow[r, 0, c:c + 1] = value[0:1]
            srow[r, 1, c:c + 1] = value[rows - 1:rows]
            low = jnp.where(lane == c, roll(value, c, 1), low)
            high = jnp.where(lane == c, roll(value, c + 1, 1), high)
        scol[r, 0] = low
        scol[r, 1] = high
        mark = len(sent)
        send(4 * r, srow.at[r, 0], rrow.at[r, 1], -1, 0)
        send(4 * r + 1, srow.at[r, 1], rrow.at[r, 0], 1, 0)
        send(4 * r + 2, scol.at[r, 0], rcol.at[r, 1], 0, -1)
        send(4 * r + 3, scol.at[r, 1], rcol.at[r, 0], 0, 1)
        return sent[mark:]

    def neighbours(r, c, value):
        up = jnp.where(row == rows - 1, rrow[r, 1, c:c + 1], roll(value, -1, 0))
        down = jnp.where(row == 0, rrow[r, 0, c:c + 1], roll(value, 1, 0))
        north = jnp.where(lane == cols - 1, roll(rcol[r, 1], cols - 1 - c, 1), roll(value, -1, 1))
        south = jnp.where(lane == 0, roll(rcol[r, 0], -c, 1), roll(value, 1, 1))
        return up, down, north, south

    loads[0].wait()
    group = send_edges(0, lambda c: vc[c, 0])
    for copy in loads[1:6]:
        copy.wait()
    boost = BOOST * vwell[...].astype(jnp.float32)
    vd[0, 0] = vd[0, 0] + boost
    center = zero
    rhs = zero
    for c in range(nc):
        center = center + vw[c] * vd[c, 0]
        rhs = rhs + vw[c] * vb[c]
    sown[0] = center
    sown[5] = rhs
    receive(group)
    links = [zero] * 4
    for c in range(nc):
        for d, value in enumerate(neighbours(0, c, vc[c, 0])):
            value = vt[d] * value
            coup[d, c] = value
            links[d] = links[d] - vw[c] * value
    for d in range(4):
        sown[1 + d] = links[d]

    for side in range(2):
        for i in range(6):
            spack[side, i] = pack(sown[i], side)
    mark = len(sent)
    for n, (dx, dy) in enumerate(SIDES):
        if dx:
            send(12 + n, sown, rx.at[(1 - dx) // 2], dx, dy)
        else:
            send(12 + n, spack.at[(1 + dy) // 2], ry.at[(1 - dy) // 2], dx, dy)
    for n, (dx, dy) in enumerate(CORNERS):
        send(16 + n, spack.at[(1 + dy) // 2], rd.at[3 - n], dx, dy)
    group = sent[mark:]

    loads[6].wait()
    for c in range(1, nc):
        vd[c, c] = vd[c, c] + boost

    def invert(step, carry):
        at = pl.ds(pl.multiple_of(step * 8, 8), 8)
        for i in range(nc):
            for j in range(nc):
                inv[i, j, at] = vd[i, j, at]
        for p in range(nc):
            reciprocal = 1.0 / inv[p, p, at]
            scaled = [reciprocal if j == p else inv[p, j, at] * reciprocal for j in range(nc)]
            for j in range(nc):
                inv[p, j, at] = scaled[j]
            for i in range(nc):
                if i != p:
                    factor = inv[i, p, at]
                    for j in range(nc):
                        if j == p:
                            inv[i, j, at] = -factor * scaled[j]
                        else:
                            inv[i, j, at] = inv[i, j, at] - factor * scaled[j]
        return carry

    lax.fori_loop(0, rows // 8, invert, 0)
    receive(group)

    for i in range(6):
        fill = 1.0 if i == 0 else 0.0
        for block in range(3):
            own = (rx[0, i], sown[i], rx[1, i])[block]
            left = (rd[0, i], ry[0, i], rd[2, i])[block]
            right = (rd[1, i], ry[1, i], rd[3, i])[block]
            halo = unpack(left, right, fill)
            target = fext if i == 5 else ext.at[i]
            target[block * rows:(block + 1) * rows, 0:cols] = own
            target[block * rows:(block + 1) * rows, cols:2 * cols] = halo

    wide = (3 * rows, 2 * cols)
    wrow = lax.broadcasted_iota(jnp.int32, wide, 0)
    wlane = lax.broadcasted_iota(jnp.int32, wide, 1)

    def aggregate(x, s):
        x = x + jnp.where((wrow & s) == 0, roll(x, -s, 0), roll(x, s, 0))
        return x + jnp.where((wlane & s) == 0, roll(x, -s, 1), roll(x, s, 1))

    def around(x, s):
        return roll(x, -s, 0), roll(x, s, 0), roll(x, -s, 1), roll(x, s, 1)

    level = [ext[i] for i in range(5)]
    for k in range(3):
        ratio = RELAX / level[0]
        recip[k] = ratio
        for d in range(4):
            (scaled0, scaled1, scaled2)[k][d] = ratio * level[1 + d]
            if k < 2:
                (link0, link1)[k][d] = level[1 + d]
        if k < 2:
            s = 1 << k
            even_x, even_y = (wrow & s) == 0, (wlane & s) == 0
            c0, east, west, north, south = level
            level = [
                aggregate(c0 + jnp.where(even_x, east, west) + jnp.where(even_y, north, south), s),
                aggregate(jnp.where(even_x, 0.0, east), s),
                aggregate(jnp.where(even_x, west, 0.0), s),
                aggregate(jnp.where(even_y, 0.0, north), s),
                aggregate(jnp.where(even_y, south, 0.0), s),
            ]

    def gather_links(coeffs, x, s):
        total = None
        for d, value in enumerate(around(x, s)):
            term = coeffs[d] * value
            total = term if total is None else total + term
        return total

    def vcycle():
        f0 = fext[...]
        g0 = recip[0] * f0
        f1 = aggregate(KEEP * f0 - gather_links(link0, g0, 1), 1)
        g1 = recip[1] * f1
        f2 = aggregate(KEEP * f1 - gather_links(link1, g1, 2), 2)
        g2 = recip[2] * f2
        e2 = g2
        for _ in range(COARSE_SWEEPS - 1):
            e2 = KEEP * e2 + g2 - gather_links(scaled2, e2, 4)
        e1 = g1 + e2
        e1 = KEEP * e1 + g1 - gather_links(scaled1, e1, 2)
        e0 = g0 + e1
        fext[...] = KEEP * e0 + g0 - gather_links(scaled0, e0, 1)
        e0 = fext[...]
        return tuple(x[rows:2 * rows, 0:cols] for x in (e0,) + around(e0, 1))

    def precondition(source, target):
        p = vcycle()
        for c in range(nc):
            total = source[c] - vd[c, 0] * p[0]
            for d in range(4):
                total = total + coup[d, c] * p[1 + d]
            prod[c] = total
        for c in range(nc):
            total = p[0] if c == 0 else zero
            for k in range(nc):
                total = total + inv[c, k] * prod[k]
            target[c] = total

    def operate(r, source, target):
        for c in range(nc):
            total = vc[c, 0] * source[0]
            for k in range(1, nc):
                total = total + vc[c, k] * source[k]
            prod[c] = total
        group = send_edges(r, lambda c: prod[c])
        for c in range(nc):
            total = vd[c, 0] * source[0]
            for k in range(1, nc):
                total = total + vd[c, k] * source[k]
            target[c] = total
        receive(group)
        for c in range(nc):
            total = target[c]
            for d, value in enumerate(neighbours(r, c, prod[c])):
                total = total - vt[d] * value
            target[c] = total

    def dot(x, y):
        total = zero
        for c in range(nc):
            total = total + x(c) * y(c)
        return jnp.sum(total, axis=0, keepdims=True)

    def part_copy(n, d):
        target = lax.rem(me + d, count)
        return pltpu.make_async_remote_copy(
            src_ref=sred.at[n], dst_ref=redall.at[n, me], send_sem=rsend.at[n, d - 1],
            recv_sem=rrecv.at[n, d - 1], device_id=(lax.div(target, gy), lax.rem(target, gy)),
            device_id_type=MESH)

    def start_reduce(n, parts):
        sred[n] = jnp.zeros(sred.shape[1:], jnp.float32)
        for i, part in enumerate(parts):
            sred[n, i:i + 1] = part

        def start(d, carry):
            part_copy(n, d).start()
            return carry

        lax.fori_loop(1, count, start, 0)
        redall[n, me] = sred[n]

    def reduced(n):
        def finish(d, carry):
            part_copy(n, d).wait()
            return carry

        lax.fori_loop(1, count, finish, 0)
        total = lax.fori_loop(1, count, lambda i, t: t + redall[n, i], redall[n, 0])
        total = jnp.sum(total, axis=1, keepdims=True)
        return total[0:1], total[1:2], total[2:3]

    precondition(vb, z1)
    loads[7].wait()
    operate(1, z1, w1)

    rhs = zero
    for c in range(nc):
        rhs = rhs + vw[c] * w1[c]
    sf[...] = rhs
    for side in range(2):
        sfp[side] = pack(rhs, side)
    mark = len(sent)
    for n, (dx, dy) in enumerate(SIDES):
        if dx:
            send(20 + n, sf, rfx.at[(1 - dx) // 2], dx, dy)
        else:
            send(20 + n, sfp.at[(1 + dy) // 2], rfy.at[(1 - dy) // 2], dx, dy)
    for n, (dx, dy) in enumerate(CORNERS):
        send(24 + n, sfp.at[(1 + dy) // 2], rfd.at[3 - n], dx, dy)
    group = sent[mark:]
    start_reduce(0, [
        dot(lambda c: vb[c], lambda c: vb[c]),
        dot(lambda c: vb[c], lambda c: w1[c]),
        dot(lambda c: w1[c], lambda c: w1[c]),
    ])
    receive(group)
    for block in range(3):
        own = (rfx[0], sf[...], rfx[1])[block]
        left = (rfd[0], rfy[0], rfd[2])[block]
        right = (rfd[1], rfy[1], rfd[3])[block]
        fext[block * rows:(block + 1) * rows, 0:cols] = own
        fext[block * rows:(block + 1) * rows, cols:2 * cols] = unpack(left, right, 0.0)
    precondition(w1, q1)
    operate(2, q1, vout)

    bb, bw, ww = reduced(0)
    beta = jnp.sqrt(bb)
    h11 = bw / bb
    h21 = jnp.sqrt(ww / bb - h11 * h11)
    scale = 1.0 / (beta * h21)
    over = 1.0 / beta

    def mapped(c):
        return (vout[c] - h11 * w1[c]) * scale

    def basis2(c):
        return (w1[c] - h11 * vb[c]) * scale

    start_reduce(1, [
        dot(mapped, lambda c: vb[c] * over),
        dot(mapped, basis2),
        dot(mapped, mapped),
    ])
    h12, h22, squared = reduced(1)
    h32 = jnp.sqrt(squared - h12 * h12 - h22 * h22)

    radius1 = jnp.sqrt(h11 * h11 + h21 * h21)
    cos1, sin1 = h11 / radius1, h21 / radius1
    top, low = cos1 * h12 + sin1 * h22, -sin1 * h12 + cos1 * h22
    radius2 = jnp.sqrt(low * low + h32 * h32)
    cos2, sin2 = low / radius2, h32 / radius2
    g0, g1 = cos1 * beta, -sin1 * beta
    g1, g2 = cos2 * g1, -sin2 * g1
    y2 = g1 / radius2
    y1 = (g0 - top * y2) / radius1
    est_ref[...] = jnp.abs(g2)
    second = y2 * scale
    first = y1 * over - second * h11
    for c in range(nc):
        out_hbm[c] = first * z1[c] + second * q1[c]

    for k, src, dst, dx, dy in sent:
        @pl.when(has[(dx, dy)])
        def _(k=k, src=src, dst=dst, dx=dx, dy=dy):
            describe(k, src, dst, dx, dy).wait_send()


def on_device(gx, gy, right_side, diag, couple, trans, weights, well):
    nc, rows, cols = right_side.shape
    f32 = jnp.float32
    wide = (3 * rows, 2 * cols)
    vm = lambda *shape: pltpu.VMEM(shape, f32)
    dma = lambda *shape: pltpu.SemaphoreType.DMA(shape)
    field = (nc, rows, cols)
    pad = -(-nc // 8) * 8
    out, est = pl.pallas_call(
        functools.partial(kernel, gx, gy),
        name="cpr_gmres",
        out_shape=(jax.ShapeDtypeStruct(field, f32), jax.ShapeDtypeStruct((1, 1), f32)),
        in_specs=[pl.BlockSpec(memory_space=pltpu.HBM)] * 6,
        out_specs=(pl.BlockSpec(memory_space=pltpu.VMEM), pl.BlockSpec(memory_space=pltpu.VMEM)),
        scratch_shapes=[
            vm(*field), vm(nc, *field), vm(nc, *field), vm(4, rows, cols), vm(*field),
            pltpu.VMEM((rows, cols), jnp.int32), vm(nc, *field), vm(4, *field),
            vm(*field), vm(*field), vm(*field), vm(*field),
            vm(3, 2, pad, cols), vm(3, 2, pad, cols), vm(3, 2, rows, cols), vm(3, 2, rows, cols),
            vm(6, rows, cols), vm(2, 6, 8, cols), vm(2, 6, rows, cols), vm(2, 6, 8, cols),
            vm(4, 6, 8, cols), vm(rows, cols), vm(2, 8, cols), vm(2, rows, cols), vm(2, 8, cols),
            vm(4, 8, cols),
            vm(5, *wide), vm(4, *wide), vm(4, *wide), vm(4, *wide), vm(4, *wide),
            vm(4, *wide), vm(3, *wide), vm(*wide), vm(*field),
            vm(2, 8, cols), vm(2, gx * gy, 8, cols),
            dma(8), dma(28), dma(28), dma(2, gx * gy - 1), dma(2, gx * gy - 1),
        ],
        compiler_params=pltpu.CompilerParams(
            collective_id=0, has_side_effects=True, vmem_limit_bytes=60 << 20),
    )(right_side, diag, couple, trans, weights, well)
    return out, est.reshape(())


def solution(mesh):
    return jax.shard_map(
        functools.partial(on_device, mesh.shape["gx"], mesh.shape["gy"]),
        mesh=mesh,
        in_specs=(
            P(None, "gx", "gy"),
            P(None, None, "gx", "gy"),
            P(None, None, "gx", "gy"),
            P(None, "gx", "gy"),
            P(None, "gx", "gy"),
            P("gx", "gy"),
        ),
        out_specs=(P(None, "gx", "gy"), P()),
        check_vma=False,
    )
```

```python
import functools

import jax
import jax.numpy as jnp
from jax import lax
from jax.experimental import pallas as pl
from jax.experimental.pallas import tpu as pltpu
from jax.sharding import PartitionSpec as P

COARSE_SWEEPS = 6
RELAX = 0.8
KEEP = 1.0 - RELAX
BOOST = 8.0
MESH = pl.DeviceIdType.MESH
PIECE = 32
SIDES = ((-1, 0), (1, 0), (0, -1), (0, 1))
CORNERS = ((-1, -1), (-1, 1), (1, -1), (1, 1))


def roll(x, shift, axis):
    shift = shift % x.shape[axis]
    return x if shift == 0 else pltpu.roll(x, shift, axis)


def kernel(gx, gy, b_hbm, diag_hbm, couple_hbm, trans_hbm, weights_hbm, well_hbm, out_hbm, est_ref,
           vb, vd, vc, vt, vw, vwell, inv, coup, prod, z1, w1, q1, srow, rrow, scol, rcol,
           sown, spack, rx, ry, rd, sf, sfp, rfx, rfy, rfd, ext, link0, scaled0, link1, scaled1,
           scaled2, recip, fext, vout, sred, redy, redx, redall,
           in_sem, ssem, rsem, ysend, yrecv, xsend, xrecv, rsend, rrecv):
    nc, rows, cols = vb.shape
    ix, iy = lax.axis_index("gx"), lax.axis_index("gy")
    has = {(-1, 0): ix > 0, (1, 0): ix < gx - 1, (0, -1): iy > 0, (0, 1): iy < gy - 1}
    for dx, dy in CORNERS:
        has[(dx, dy)] = jnp.logical_and(has[(dx, 0)], has[(0, dy)])

    loads = []
    for n, (src, dst) in enumerate((
        (couple_hbm.at[:, 0], vc.at[:, 0]),
        (weights_hbm, vw),
        (trans_hbm, vt),
        (b_hbm, vb),
        (well_hbm, vwell),
        (diag_hbm.at[:, 0], vd.at[:, 0]),
        (diag_hbm.at[:, pl.ds(1, nc - 1)], vd.at[:, pl.ds(1, nc - 1)]),
        (couple_hbm.at[:, pl.ds(1, nc - 1)], vc.at[:, pl.ds(1, nc - 1)]),
    )):
        copy = pltpu.make_async_copy(src, dst, in_sem.at[n])
        copy.start()
        loads.append(copy)

    row = lax.broadcasted_iota(jnp.int32, (rows, cols), 0)
    lane = lax.broadcasted_iota(jnp.int32, (rows, cols), 1)
    zero = jnp.zeros((rows, cols), jnp.float32)
    ones = jnp.ones((rows, cols), jnp.float32)

    blank = jnp.zeros((8, cols), jnp.float32)
    for s in range(2):
        for i in range(6):
            rx[s, i] = ones if i == 0 else zero
            ry[s, i] = blank + 1.0 if i == 0 else blank
        rfx[s] = zero
        rfy[s] = blank
        for r in range(3):
            rrow[r, s] = jnp.zeros(rrow.shape[2:], jnp.float32)
            rcol[r, s] = zero
    for s in range(4):
        for i in range(6):
            rd[s, i] = blank + 1.0 if i == 0 else blank
        rfd[s] = blank

    barrier = pltpu.get_barrier_semaphore()
    count = gx * gy
    me = ix * gy + iy

    for d in range(1, gy):
        pl.semaphore_signal(barrier, inc=1, device_id=(ix, lax.rem(iy + d, gy)), device_id_type=MESH)
    for d in range(1, gx):
        pl.semaphore_signal(barrier, inc=1, device_id=(lax.rem(ix + d, gx), iy), device_id_type=MESH)
    for dx, dy in CORNERS:
        @pl.when(has[(dx, dy)])
        def _(dx=dx, dy=dy):
            pl.semaphore_signal(barrier, inc=1, device_id=(ix + dx, iy + dy), device_id_type=MESH)
    near_x = has[(-1, 0)].astype(jnp.int32) + has[(1, 0)].astype(jnp.int32)
    near_y = has[(0, -1)].astype(jnp.int32) + has[(0, 1)].astype(jnp.int32)
    pl.semaphore_wait(barrier, gx + gy - 2 + near_x * near_y)

    groups = rows // 8
    tile_lane = lane[0:8]

    def pack(plane, side):
        tile = jnp.zeros((8, cols), jnp.float32)
        for j in range(groups):
            inside = jnp.logical_and(tile_lane >= PIECE * j, tile_lane < PIECE * (j + 1))
            tile = jnp.where(inside, roll(plane[8 * j:8 * j + 8], PIECE * (j + side), 1), tile)
        return tile

    def unpack(left, right, fill):
        parts = []
        for j in range(groups):
            first = roll(right, -PIECE * j, 1)
            last = roll(left, -PIECE * (j + 1), 1)
            parts.append(jnp.where(tile_lane < PIECE, first,
                                   jnp.where(tile_lane >= cols - PIECE, last, fill)))
        return jnp.concatenate(parts, axis=0)

    sent = []

    def describe(k, src, dst, dx, dy):
        return pltpu.make_async_remote_copy(
            src_ref=src, dst_ref=dst, send_sem=ssem.at[k], recv_sem=rsem.at[k],
            device_id=(ix + dx, iy + dy), device_id_type=MESH)

    def send(k, src, dst, dx, dy):
        @pl.when(has[(dx, dy)])
        def _():
            describe(k, src, dst, dx, dy).start()
        sent.append((k, src, dst, dx, dy))

    def receive(group):
        for k, src, dst, dx, dy in group:
            @pl.when(has[(-dx, -dy)])
            def _(k=k, src=src, dst=dst, dx=dx, dy=dy):
                describe(k, src, dst, dx, dy).wait_recv()

    def send_edges(r, plane):
        low, high = zero, zero
        for c in range(nc):
            value = plane(c)
            srow[r, 0, c:c + 1] = value[0:1]
            srow[r, 1, c:c + 1] = value[rows - 1:rows]
            low = jnp.where(lane == c, roll(value, c, 1), low)
            high = jnp.where(lane == c, roll(value, c + 1, 1), high)
        scol[r, 0] = low
        scol[r, 1] = high
        mark = len(sent)
        send(4 * r, srow.at[r, 0], rrow.at[r, 1], -1, 0)
        send(4 * r + 1, srow.at[r, 1], rrow.at[r, 0], 1, 0)
        send(4 * r + 2, scol.at[r, 0], rcol.at[r, 1], 0, -1)
        send(4 * r + 3, scol.at[r, 1], rcol.at[r, 0], 0, 1)
        return sent[mark:]

    def neighbours(r, c, value):
        up = jnp.where(row == rows - 1, rrow[r, 1, c:c + 1], roll(value, -1, 0))
        down = jnp.where(row == 0, rrow[r, 0, c:c + 1], roll(value, 1, 0))
        north = jnp.where(lane == cols - 1, roll(rcol[r, 1], cols - 1 - c, 1), roll(value, -1, 1))
        south = jnp.where(lane == 0, roll(rcol[r, 0], -c, 1), roll(value, 1, 1))
        return up, down, north, south

    loads[0].wait()
    group = send_edges(0, lambda c: vc[c, 0])
    for copy in loads[1:6]:
        copy.wait()
    boost = BOOST * vwell[...].astype(jnp.float32)
    vd[0, 0] = vd[0, 0] + boost
    center = zero
    rhs = zero
    for c in range(nc):
        center = center + vw[c] * vd[c, 0]
        rhs = rhs + vw[c] * vb[c]
    sown[0] = center
    sown[5] = rhs
    receive(group)
    links = [zero] * 4
    for c in range(nc):
        for d, value in enumerate(neighbours(0, c, vc[c, 0])):
            value = vt[d] * value
            coup[d, c] = value
            links[d] = links[d] - vw[c] * value
    for d in range(4):
        sown[1 + d] = links[d]

    for side in range(2):
        for i in range(6):
            spack[side, i] = pack(sown[i], side)
    mark = len(sent)
    for n, (dx, dy) in enumerate(SIDES):
        if dx:
            send(12 + n, sown, rx.at[(1 - dx) // 2], dx, dy)
        else:
            send(12 + n, spack.at[(1 + dy) // 2], ry.at[(1 - dy) // 2], dx, dy)
    for n, (dx, dy) in enumerate(CORNERS):
        send(16 + n, spack.at[(1 + dy) // 2], rd.at[3 - n], dx, dy)
    group = sent[mark:]

    loads[6].wait()
    for c in range(1, nc):
        vd[c, c] = vd[c, c] + boost

    def invert(step, carry):
        at = pl.ds(pl.multiple_of(step * 8, 8), 8)
        for i in range(nc):
            for j in range(nc):
                inv[i, j, at] = vd[i, j, at]
        for p in range(nc):
            reciprocal = 1.0 / inv[p, p, at]
            scaled = [reciprocal if j == p else inv[p, j, at] * reciprocal for j in range(nc)]
            for j in range(nc):
                inv[p, j, at] = scaled[j]
            for i in range(nc):
                if i != p:
                    factor = inv[i, p, at]
                    for j in range(nc):
                        if j == p:
                            inv[i, j, at] = -factor * scaled[j]
                        else:
                            inv[i, j, at] = inv[i, j, at] - factor * scaled[j]
        return carry

    lax.fori_loop(0, rows // 8, invert, 0)
    receive(group)

    for i in range(6):
        fill = 1.0 if i == 0 else 0.0
        for block in range(3):
            own = (rx[0, i], sown[i], rx[1, i])[block]
            left = (rd[0, i], ry[0, i], rd[2, i])[block]
            right = (rd[1, i], ry[1, i], rd[3, i])[block]
            halo = unpack(left, right, fill)
            target = fext if i == 5 else ext.at[i]
            target[block * rows:(block + 1) * rows, 0:cols] = own
            target[block * rows:(block + 1) * rows, cols:2 * cols] = halo

    wide = (3 * rows, 2 * cols)
    wrow = lax.broadcasted_iota(jnp.int32, wide, 0)
    wlane = lax.broadcasted_iota(jnp.int32, wide, 1)

    def aggregate(x, s):
        x = x + jnp.where((wrow & s) == 0, roll(x, -s, 0), roll(x, s, 0))
        return x + jnp.where((wlane & s) == 0, roll(x, -s, 1), roll(x, s, 1))

    def around(x, s):
        return roll(x, -s, 0), roll(x, s, 0), roll(x, -s, 1), roll(x, s, 1)

    level = [ext[i] for i in range(5)]
    for k in range(3):
        ratio = RELAX / level[0]
        recip[k] = ratio
        for d in range(4):
            (scaled0, scaled1, scaled2)[k][d] = ratio * level[1 + d]
            if k < 2:
                (link0, link1)[k][d] = level[1 + d]
        if k < 2:
            s = 1 << k
            even_x, even_y = (wrow & s) == 0, (wlane & s) == 0
            c0, east, west, north, south = level
            level = [
                aggregate(c0 + jnp.where(even_x, east, west) + jnp.where(even_y, north, south), s),
                aggregate(jnp.where(even_x, 0.0, east), s),
                aggregate(jnp.where(even_x, west, 0.0), s),
                aggregate(jnp.where(even_y, 0.0, north), s),
                aggregate(jnp.where(even_y, south, 0.0), s),
            ]

    def gather_links(coeffs, x, s):
        total = None
        for d, value in enumerate(around(x, s)):
            term = coeffs[d] * value
            total = term if total is None else total + term
        return total

    def vcycle():
        f0 = fext[...]
        g0 = recip[0] * f0
        f1 = aggregate(KEEP * f0 - gather_links(link0, g0, 1), 1)
        g1 = recip[1] * f1
        f2 = aggregate(KEEP * f1 - gather_links(link1, g1, 2), 2)
        g2 = recip[2] * f2
        e2 = g2
        for _ in range(COARSE_SWEEPS - 1):
            e2 = KEEP * e2 + g2 - gather_links(scaled2, e2, 4)
        e1 = g1 + e2
        e1 = KEEP * e1 + g1 - gather_links(scaled1, e1, 2)
        e0 = g0 + e1
        fext[...] = KEEP * e0 + g0 - gather_links(scaled0, e0, 1)
        e0 = fext[...]
        return tuple(x[rows:2 * rows, 0:cols] for x in (e0,) + around(e0, 1))

    def precondition(source, target):
        p = vcycle()
        for c in range(nc):
            total = source[c] - vd[c, 0] * p[0]
            for d in range(4):
                total = total + coup[d, c] * p[1 + d]
            prod[c] = total
        for c in range(nc):
            total = p[0] if c == 0 else zero
            for k in range(nc):
                total = total + inv[c, k] * prod[k]
            target[c] = total

    def operate(r, source, target):
        for c in range(nc):
            total = vc[c, 0] * source[0]
            for k in range(1, nc):
                total = total + vc[c, k] * source[k]
            prod[c] = total
        group = send_edges(r, lambda c: prod[c])
        for c in range(nc):
            total = vd[c, 0] * source[0]
            for k in range(1, nc):
                total = total + vd[c, k] * source[k]
            target[c] = total
        receive(group)
        for c in range(nc):
            total = target[c]
            for d, value in enumerate(neighbours(r, c, prod[c])):
                total = total - vt[d] * value
            target[c] = total

    def dot(x, y):
        total = zero
        for c in range(nc):
            total = total + x(c) * y(c)
        return jnp.sum(total, axis=0, keepdims=True)

    def line_copies(axis, src, dst, send_sems, recv_sems):
        copies = []
        for d in range(1, (gx, gy)[axis]):
            if axis:
                target = (ix, lax.rem(iy + d, gy))
            else:
                target = (lax.rem(ix + d, gx), iy)
            copies.append(pltpu.make_async_remote_copy(
                src_ref=src, dst_ref=dst.at[(ix, iy)[axis]], send_sem=send_sems.at[d - 1],
                recv_sem=recv_sems.at[d - 1], device_id=target, device_id_type=MESH))
        return copies

    def fill(parts, n):
        sred[n] = jnp.zeros(sred.shape[1:], jnp.float32)
        for i, part in enumerate(parts):
            sred[n, i:i + 1] = part

    def finish_sum(total):
        total = jnp.sum(total, axis=1, keepdims=True)
        return total[0:1], total[1:2], total[2:3]

    def start_lines(parts):
        fill(parts, 0)
        copies = line_copies(1, sred.at[0], redy, ysend, yrecv)
        for copy in copies:
            copy.start()
        redy[iy] = sred[0]
        return copies

    def turn_lines(copies):
        for copy in copies:
            copy.wait()
        total = redy[0]
        for i in range(1, gy):
            total = total + redy[i]
        sred[1] = total
        copies = line_copies(0, sred.at[1], redx, xsend, xrecv)
        for copy in copies:
            copy.start()
        redx[ix] = total
        return copies

    def end_lines(copies):
        for copy in copies:
            copy.wait()
        total = redx[0]
        for i in range(1, gx):
            total = total + redx[i]
        return finish_sum(total)

    def part_copy(d):
        target = lax.rem(me + d, count)
        return pltpu.make_async_remote_copy(
            src_ref=sred.at[2], dst_ref=redall.at[me], send_sem=rsend.at[d - 1],
            recv_sem=rrecv.at[d - 1], device_id=(lax.div(target, gy), lax.rem(target, gy)),
            device_id_type=MESH)

    def reduce_all(parts):
        fill(parts, 2)

        def start(d, carry):
            part_copy(d).start()
            return carry

        def finish(d, carry):
            part_copy(d).wait()
            return carry

        lax.fori_loop(1, count, start, 0)
        redall[me] = sred[2]
        lax.fori_loop(1, count, finish, 0)
        total = redall[0]
        for i in range(1, count):
            total = total + redall[i]
        return finish_sum(total)

    precondition(vb, z1)
    loads[7].wait()
    operate(1, z1, w1)

    rhs = zero
    for c in range(nc):
        rhs = rhs + vw[c] * w1[c]
    sf[...] = rhs
    for side in range(2):
        sfp[side] = pack(rhs, side)
    mark = len(sent)
    for n, (dx, dy) in enumerate(SIDES):
        if dx:
            send(20 + n, sf, rfx.at[(1 - dx) // 2], dx, dy)
        else:
            send(20 + n, sfp.at[(1 + dy) // 2], rfy.at[(1 - dy) // 2], dx, dy)
    for n, (dx, dy) in enumerate(CORNERS):
        send(24 + n, sfp.at[(1 + dy) // 2], rfd.at[3 - n], dx, dy)
    group = sent[mark:]
    copies = start_lines([
        dot(lambda c: vb[c], lambda c: vb[c]),
        dot(lambda c: vb[c], lambda c: w1[c]),
        dot(lambda c: w1[c], lambda c: w1[c]),
    ])
    receive(group)
    for block in range(3):
        own = (rfx[0], sf[...], rfx[1])[block]
        left = (rfd[0], rfy[0], rfd[2])[block]
        right = (rfd[1], rfy[1], rfd[3])[block]
        fext[block * rows:(block + 1) * rows, 0:cols] = own
        fext[block * rows:(block + 1) * rows, cols:2 * cols] = unpack(left, right, 0.0)
    precondition(w1, q1)
    copies = turn_lines(copies)
    operate(2, q1, vout)

    bb, bw, ww = end_lines(copies)
    beta = jnp.sqrt(bb)
    h11 = bw / bb
    h21 = jnp.sqrt(ww / bb - h11 * h11)
    scale = 1.0 / (beta * h21)
    over = 1.0 / beta

    def mapped(c):
        return (vout[c] - h11 * w1[c]) * scale

    def basis2(c):
        return (w1[c] - h11 * vb[c]) * scale

    h12, h22, squared = reduce_all([
        dot(mapped, lambda c: vb[c] * over),
        dot(mapped, basis2),
        dot(mapped, mapped),
    ])
    h32 = jnp.sqrt(squared - h12 * h12 - h22 * h22)

    radius1 = jnp.sqrt(h11 * h11 + h21 * h21)
    cos1, sin1 = h11 / radius1, h21 / radius1
    top, low = cos1 * h12 + sin1 * h22, -sin1 * h12 + cos1 * h22
    radius2 = jnp.sqrt(low * low + h32 * h32)
    cos2, sin2 = low / radius2, h32 / radius2
    g0, g1 = cos1 * beta, -sin1 * beta
    g1, g2 = cos2 * g1, -sin2 * g1
    y2 = g1 / radius2
    y1 = (g0 - top * y2) / radius1
    est_ref[...] = jnp.abs(g2)
    second = y2 * scale
    first = y1 * over - second * h11
    for c in range(nc):
        out_hbm[c] = first * z1[c] + second * q1[c]

    for k, src, dst, dx, dy in sent:
        @pl.when(has[(dx, dy)])
        def _(k=k, src=src, dst=dst, dx=dx, dy=dy):
            describe(k, src, dst, dx, dy).wait_send()


def on_device(gx, gy, right_side, diag, couple, trans, weights, well):
    nc, rows, cols = right_side.shape
    f32 = jnp.float32
    wide = (3 * rows, 2 * cols)
    vm = lambda *shape: pltpu.VMEM(shape, f32)
    dma = lambda *shape: pltpu.SemaphoreType.DMA(shape)
    field = (nc, rows, cols)
    pad = -(-nc // 8) * 8
    out, est = pl.pallas_call(
        functools.partial(kernel, gx, gy),
        name="cpr_gmres",
        out_shape=(jax.ShapeDtypeStruct(field, f32), jax.ShapeDtypeStruct((1, 1), f32)),
        in_specs=[pl.BlockSpec(memory_space=pltpu.HBM)] * 6,
        out_specs=(pl.BlockSpec(memory_space=pltpu.VMEM), pl.BlockSpec(memory_space=pltpu.VMEM)),
        scratch_shapes=[
            vm(*field), vm(nc, *field), vm(nc, *field), vm(4, rows, cols), vm(*field),
            pltpu.VMEM((rows, cols), jnp.int32), vm(nc, *field), vm(4, *field),
            vm(*field), vm(*field), vm(*field), vm(*field),
            vm(3, 2, pad, cols), vm(3, 2, pad, cols), vm(3, 2, rows, cols), vm(3, 2, rows, cols),
            vm(6, rows, cols), vm(2, 6, 8, cols), vm(2, 6, rows, cols), vm(2, 6, 8, cols),
            vm(4, 6, 8, cols), vm(rows, cols), vm(2, 8, cols), vm(2, rows, cols), vm(2, 8, cols),
            vm(4, 8, cols),
            vm(5, *wide), vm(4, *wide), vm(4, *wide), vm(4, *wide), vm(4, *wide),
            vm(4, *wide), vm(3, *wide), vm(*wide), vm(*field),
            vm(3, 8, cols), vm(gy, 8, cols), vm(gx, 8, cols), vm(gx * gy, 8, cols),
            dma(8), dma(28), dma(28), dma(gy - 1), dma(gy - 1), dma(gx - 1), dma(gx - 1),
            dma(gx * gy - 1), dma(gx * gy - 1),
        ],
        compiler_params=pltpu.CompilerParams(
            collective_id=0, has_side_effects=True, vmem_limit_bytes=60 << 20),
    )(right_side, diag, couple, trans, weights, well)
    return out, est.reshape(())


def solution(mesh):
    return jax.shard_map(
        functools.partial(on_device, mesh.shape["gx"], mesh.shape["gy"]),
        mesh=mesh,
        in_specs=(
            P(None, "gx", "gy"),
            P(None, None, "gx", "gy"),
            P(None, None, "gx", "gy"),
            P(None, "gx", "gy"),
            P(None, "gx", "gy"),
            P("gx", "gy"),
        ),
        out_specs=(P(None, "gx", "gy"), P()),
        check_vma=False,
    )
```

```python
import functools

import jax
import jax.numpy as jnp
from jax import lax
from jax.experimental import pallas as pl
from jax.experimental.pallas import tpu as pltpu
from jax.sharding import PartitionSpec as P

COARSE_SWEEPS = 6
RELAX = 0.8
KEEP = 1.0 - RELAX
BOOST = 8.0
MESH = pl.DeviceIdType.MESH
PIECE = 32
SIDES = ((-1, 0), (1, 0), (0, -1), (0, 1))
CORNERS = ((-1, -1), (-1, 1), (1, -1), (1, 1))


def roll(x, shift, axis):
    shift = shift % x.shape[axis]
    return x if shift == 0 else pltpu.roll(x, shift, axis)


def kernel(gx, gy, b_hbm, diag_hbm, couple_hbm, trans_hbm, weights_hbm, well_hbm, out_hbm, est_ref,
           vb, vd, vc, vt, vw, vwell, inv, coup, prod, z1, w1, q1, srow, rrow, scol, rcol,
           sown, spack, rx, ry, rd, sf, sfp, sfix, rfix, lown, rfx, rfy, rfd, ext, link0, scaled0, link1, scaled1,
           scaled2, recip, fext, vout, sred, redy, redx, redall,
           in_sem, ssem, rsem, ysend, yrecv, xsend, xrecv, rsend, rrecv):
    nc, rows, cols = vb.shape
    ix, iy = lax.axis_index("gx"), lax.axis_index("gy")
    has = {(-1, 0): ix > 0, (1, 0): ix < gx - 1, (0, -1): iy > 0, (0, 1): iy < gy - 1}
    for dx, dy in CORNERS:
        has[(dx, dy)] = jnp.logical_and(has[(dx, 0)], has[(0, dy)])

    loads = []
    for n, (src, dst) in enumerate((
        (couple_hbm.at[:, 0], vc.at[:, 0]),
        (weights_hbm, vw),
        (trans_hbm, vt),
        (b_hbm, vb),
        (well_hbm, vwell),
        (diag_hbm.at[:, 0], vd.at[:, 0]),
        (diag_hbm.at[:, pl.ds(1, nc - 1)], vd.at[:, pl.ds(1, nc - 1)]),
        (couple_hbm.at[:, pl.ds(1, nc - 1)], vc.at[:, pl.ds(1, nc - 1)]),
    )):
        copy = pltpu.make_async_copy(src, dst, in_sem.at[n])
        copy.start()
        loads.append(copy)

    row = lax.broadcasted_iota(jnp.int32, (rows, cols), 0)
    lane = lax.broadcasted_iota(jnp.int32, (rows, cols), 1)
    zero = jnp.zeros((rows, cols), jnp.float32)
    ones = jnp.ones((rows, cols), jnp.float32)

    blank = jnp.zeros((8, cols), jnp.float32)
    for s in range(2):
        for i in range(6):
            rx[s, i] = ones if i == 0 else zero
            ry[s, i] = blank + 1.0 if i == 0 else blank
        rfx[s] = zero
        rfy[s] = blank
        for r in range(3):
            rrow[r, s] = jnp.zeros(rrow.shape[2:], jnp.float32)
            rcol[r, s] = zero
    for s in range(8):
        rfix[s] = blank
    for s in range(4):
        for i in range(6):
            rd[s, i] = blank + 1.0 if i == 0 else blank
        rfd[s] = blank

    barrier = pltpu.get_barrier_semaphore()
    count = gx * gy
    me = ix * gy + iy

    for d in range(1, gy):
        pl.semaphore_signal(barrier, inc=1, device_id=(ix, lax.rem(iy + d, gy)), device_id_type=MESH)
    for d in range(1, gx):
        pl.semaphore_signal(barrier, inc=1, device_id=(lax.rem(ix + d, gx), iy), device_id_type=MESH)
    for dx, dy in CORNERS:
        @pl.when(has[(dx, dy)])
        def _(dx=dx, dy=dy):
            pl.semaphore_signal(barrier, inc=1, device_id=(ix + dx, iy + dy), device_id_type=MESH)
    near_x = has[(-1, 0)].astype(jnp.int32) + has[(1, 0)].astype(jnp.int32)
    near_y = has[(0, -1)].astype(jnp.int32) + has[(0, 1)].astype(jnp.int32)
    pl.semaphore_wait(barrier, gx + gy - 2 + near_x * near_y)

    groups = rows // 8
    tile_lane = lane[0:8]

    def pack(plane, side):
        tile = jnp.zeros((8, cols), jnp.float32)
        for j in range(groups):
            inside = jnp.logical_and(tile_lane >= PIECE * j, tile_lane < PIECE * (j + 1))
            tile = jnp.where(inside, roll(plane[8 * j:8 * j + 8], PIECE * (j + side), 1), tile)
        return tile

    def unpack(left, right, fill):
        parts = []
        for j in range(groups):
            first = roll(right, -PIECE * j, 1)
            last = roll(left, -PIECE * (j + 1), 1)
            parts.append(jnp.where(tile_lane < PIECE, first,
                                   jnp.where(tile_lane >= cols - PIECE, last, fill)))
        return jnp.concatenate(parts, axis=0)

    sent = []

    def describe(k, src, dst, dx, dy):
        return pltpu.make_async_remote_copy(
            src_ref=src, dst_ref=dst, send_sem=ssem.at[k], recv_sem=rsem.at[k],
            device_id=(ix + dx, iy + dy), device_id_type=MESH)

    def send(k, src, dst, dx, dy):
        @pl.when(has[(dx, dy)])
        def _():
            describe(k, src, dst, dx, dy).start()
        sent.append((k, src, dst, dx, dy))

    def receive(group):
        for k, src, dst, dx, dy in group:
            @pl.when(has[(-dx, -dy)])
            def _(k=k, src=src, dst=dst, dx=dx, dy=dy):
                describe(k, src, dst, dx, dy).wait_recv()

    def send_edges(r, plane):
        low, high = zero, zero
        for c in range(nc):
            value = plane(c)
            srow[r, 0, c:c + 1] = value[0:1]
            srow[r, 1, c:c + 1] = value[rows - 1:rows]
            low = jnp.where(lane == c, roll(value, c, 1), low)
            high = jnp.where(lane == c, roll(value, c + 1, 1), high)
        scol[r, 0] = low
        scol[r, 1] = high
        mark = len(sent)
        send(4 * r, srow.at[r, 0], rrow.at[r, 1], -1, 0)
        send(4 * r + 1, srow.at[r, 1], rrow.at[r, 0], 1, 0)
        send(4 * r + 2, scol.at[r, 0], rcol.at[r, 1], 0, -1)
        send(4 * r + 3, scol.at[r, 1], rcol.at[r, 0], 0, 1)
        return sent[mark:]

    def neighbours(r, c, value):
        up = jnp.where(row == rows - 1, rrow[r, 1, c:c + 1], roll(value, -1, 0))
        down = jnp.where(row == 0, rrow[r, 0, c:c + 1], roll(value, 1, 0))
        north = jnp.where(lane == cols - 1, roll(rcol[r, 1], cols - 1 - c, 1), roll(value, -1, 1))
        south = jnp.where(lane == 0, roll(rcol[r, 0], -c, 1), roll(value, 1, 1))
        return up, down, north, south

    loads[0].wait()
    group = send_edges(0, lambda c: vc[c, 0])
    for copy in loads[1:6]:
        copy.wait()
    boost = BOOST * vwell[...].astype(jnp.float32)
    vd[0, 0] = vd[0, 0] + boost
    center = zero
    rhs = zero
    for c in range(nc):
        center = center + vw[c] * vd[c, 0]
        rhs = rhs + vw[c] * vb[c]
    sown[0] = center
    sown[5] = rhs
    first_edges = group
    links = [zero] * 4
    for c in range(nc):
        value = vc[c, 0]
        shifted = (jnp.where(row == rows - 1, 0.0, roll(value, -1, 0)),
                   jnp.where(row == 0, 0.0, roll(value, 1, 0)),
                   jnp.where(lane == cols - 1, 0.0, roll(value, -1, 1)),
                   jnp.where(lane == 0, 0.0, roll(value, 1, 1)))
        for d in range(4):
            links[d] = links[d] - vw[c] * (vt[d] * shifted[d])
    for d in range(4):
        sown[1 + d] = links[d]

    for side in range(2):
        for i in range(6):
            spack[side, i] = pack(sown[i], side)
    mark = len(sent)
    for n, (dx, dy) in enumerate(SIDES):
        if dx:
            send(12 + n, sown, rx.at[(1 - dx) // 2], dx, dy)
        else:
            send(12 + n, spack.at[(1 + dy) // 2], ry.at[(1 - dy) // 2], dx, dy)
    for n, (dx, dy) in enumerate(CORNERS):
        send(16 + n, spack.at[(1 + dy) // 2], rd.at[3 - n], dx, dy)
    group = sent[mark:]

    receive(first_edges)
    links = [zero] * 4
    for c in range(nc):
        for d, value in enumerate(neighbours(0, c, vc[c, 0])):
            value = vt[d] * value
            coup[d, c] = value
            links[d] = links[d] - vw[c] * value
    for d in range(4):
        lown[d] = links[d]
    sfix[...] = blank
    sfix[0:1] = links[0][rows - 1:rows]
    sfix[1:2] = links[1][0:1]
    for d, at in ((2, cols - 1), (3, 0)):
        spread = jnp.broadcast_to(links[d][:, at:at + 1], (rows, cols))
        sfix[d:d + 1] = jnp.sum(jnp.where(row == lane, spread, 0.0), axis=0, keepdims=True)
    mark = len(sent)
    for n, (dx, dy) in enumerate(SIDES + CORNERS):
        slot = n ^ 1 if n < 4 else 11 - n
        send(28 + n, sfix, rfix.at[slot], dx, dy)
    fixes = sent[mark:]

    loads[6].wait()
    for c in range(1, nc):
        vd[c, c] = vd[c, c] + boost

    def invert(step, carry):
        at = pl.ds(pl.multiple_of(step * 8, 8), 8)
        for i in range(nc):
            for j in range(nc):
                inv[i, j, at] = vd[i, j, at]
        for p in range(nc):
            reciprocal = 1.0 / inv[p, p, at]
            scaled = [reciprocal if j == p else inv[p, j, at] * reciprocal for j in range(nc)]
            for j in range(nc):
                inv[p, j, at] = scaled[j]
            for i in range(nc):
                if i != p:
                    factor = inv[i, p, at]
                    for j in range(nc):
                        if j == p:
                            inv[i, j, at] = -factor * scaled[j]
                        else:
                            inv[i, j, at] = inv[i, j, at] - factor * scaled[j]
        return carry

    lax.fori_loop(0, rows // 8, invert, 0)
    receive(group)
    receive(fixes)

    def column(slot, d):
        return jnp.sum(jnp.where(row == lane, rfix[slot, d:d + 1], 0.0), axis=1, keepdims=True)

    def mend(d, plane, left, right):
        if d < 2:
            edge = jnp.where(lane[0:1] < cols // 2, rfix[right, d:d + 1], rfix[left, d:d + 1])
            return jnp.where(row == (rows - 1, 0)[d], edge, plane)
        slot, at = ((left, cols - 1), (right, 0))[d - 2]
        return jnp.where(lane == at, column(slot, d), plane)

    for i in range(6):
        fill = 1.0 if i == 0 else 0.0
        for block in range(3):
            border = 1 <= i <= 4
            own = (rx[0, i], lown[i - 1] if border else sown[i], rx[1, i])[block]
            if border and block != 1:
                own = mend(i - 1, own, block // 2, block // 2)
            left = (rd[0, i], ry[0, i], rd[2, i])[block]
            right = (rd[1, i], ry[1, i], rd[3, i])[block]
            halo = unpack(left, right, fill)
            if border:
                halo = mend(i - 1, halo, (4, 2, 6)[block], (5, 3, 7)[block])
            target = fext if i == 5 else ext.at[i]
            target[block * rows:(block + 1) * rows, 0:cols] = own
            target[block * rows:(block + 1) * rows, cols:2 * cols] = halo

    wide = (3 * rows, 2 * cols)
    wrow = lax.broadcasted_iota(jnp.int32, wide, 0)
    wlane = lax.broadcasted_iota(jnp.int32, wide, 1)

    def aggregate(x, s):
        x = x + jnp.where((wrow & s) == 0, roll(x, -s, 0), roll(x, s, 0))
        return x + jnp.where((wlane & s) == 0, roll(x, -s, 1), roll(x, s, 1))

    def around(x, s):
        return roll(x, -s, 0), roll(x, s, 0), roll(x, -s, 1), roll(x, s, 1)

    level = [ext[i] for i in range(5)]
    for k in range(3):
        ratio = RELAX / level[0]
        recip[k] = ratio
        for d in range(4):
            (scaled0, scaled1, scaled2)[k][d] = ratio * level[1 + d]
            if k < 2:
                (link0, link1)[k][d] = level[1 + d]
        if k < 2:
            s = 1 << k
            even_x, even_y = (wrow & s) == 0, (wlane & s) == 0
            c0, east, west, north, south = level
            level = [
                aggregate(c0 + jnp.where(even_x, east, west) + jnp.where(even_y, north, south), s),
                aggregate(jnp.where(even_x, 0.0, east), s),
                aggregate(jnp.where(even_x, west, 0.0), s),
                aggregate(jnp.where(even_y, 0.0, north), s),
                aggregate(jnp.where(even_y, south, 0.0), s),
            ]

    def gather_links(coeffs, x, s):
        total = None
        for d, value in enumerate(around(x, s)):
            term = coeffs[d] * value
            total = term if total is None else total + term
        return total

    def vcycle():
        f0 = fext[...]
        g0 = recip[0] * f0
        f1 = aggregate(KEEP * f0 - gather_links(link0, g0, 1), 1)
        g1 = recip[1] * f1
        f2 = aggregate(KEEP * f1 - gather_links(link1, g1, 2), 2)
        g2 = recip[2] * f2
        e2 = g2
        for _ in range(COARSE_SWEEPS - 1):
            e2 = KEEP * e2 + g2 - gather_links(scaled2, e2, 4)
        e1 = g1 + e2
        e1 = KEEP * e1 + g1 - gather_links(scaled1, e1, 2)
        e0 = g0 + e1
        fext[...] = KEEP * e0 + g0 - gather_links(scaled0, e0, 1)
        e0 = fext[...]
        return tuple(x[rows:2 * rows, 0:cols] for x in (e0,) + around(e0, 1))

    def precondition(source, target):
        p = vcycle()
        for c in range(nc):
            total = source[c] - vd[c, 0] * p[0]
            for d in range(4):
                total = total + coup[d, c] * p[1 + d]
            prod[c] = total
        for c in range(nc):
            total = p[0] if c == 0 else zero
            for k in range(nc):
                total = total + inv[c, k] * prod[k]
            target[c] = total

    def operate(r, source, target):
        for c in range(nc):
            total = vc[c, 0] * source[0]
            for k in range(1, nc):
                total = total + vc[c, k] * source[k]
            prod[c] = total
        group = send_edges(r, lambda c: prod[c])
        for c in range(nc):
            total = vd[c, 0] * source[0]
            for k in range(1, nc):
                total = total + vd[c, k] * source[k]
            target[c] = total
        receive(group)
        for c in range(nc):
            total = target[c]
            for d, value in enumerate(neighbours(r, c, prod[c])):
                total = total - vt[d] * value
            target[c] = total

    def dot(x, y):
        total = zero
        for c in range(nc):
            total = total + x(c) * y(c)
        return jnp.sum(total, axis=0, keepdims=True)

    def line_copies(axis, src, dst, send_sems, recv_sems):
        copies = []
        for d in range(1, (gx, gy)[axis]):
            if axis:
                target = (ix, lax.rem(iy + d, gy))
            else:
                target = (lax.rem(ix + d, gx), iy)
            copies.append(pltpu.make_async_remote_copy(
                src_ref=src, dst_ref=dst.at[(ix, iy)[axis]], send_sem=send_sems.at[d - 1],
                recv_sem=recv_sems.at[d - 1], device_id=target, device_id_type=MESH))
        return copies

    def fill(parts, n):
        sred[n] = jnp.zeros(sred.shape[1:], jnp.float32)
        for i, part in enumerate(parts):
            sred[n, i:i + 1] = part

    def finish_sum(total):
        total = jnp.sum(total, axis=1, keepdims=True)
        return total[0:1], total[1:2], total[2:3]

    def start_lines(parts):
        fill(parts, 0)
        copies = line_copies(1, sred.at[0], redy, ysend, yrecv)
        for copy in copies:
            copy.start()
        redy[iy] = sred[0]
        return copies

    def turn_lines(copies):
        for copy in copies:
            copy.wait()
        total = redy[0]
        for i in range(1, gy):
            total = total + redy[i]
        sred[1] = total
        copies = line_copies(0, sred.at[1], redx, xsend, xrecv)
        for copy in copies:
            copy.start()
        redx[ix] = total
        return copies

    def end_lines(copies):
        for copy in copies:
            copy.wait()
        total = redx[0]
        for i in range(1, gx):
            total = total + redx[i]
        return finish_sum(total)

    def part_copy(d):
        target = lax.rem(me + d, count)
        return pltpu.make_async_remote_copy(
            src_ref=sred.at[2], dst_ref=redall.at[me], send_sem=rsend.at[d - 1],
            recv_sem=rrecv.at[d - 1], device_id=(lax.div(target, gy), lax.rem(target, gy)),
            device_id_type=MESH)

    def reduce_all(parts):
        fill(parts, 2)

        def start(d, carry):
            part_copy(d).start()
            return carry

        def finish(d, carry):
            part_copy(d).wait()
            return carry

        lax.fori_loop(1, count, start, 0)
        redall[me] = sred[2]
        lax.fori_loop(1, count, finish, 0)
        total = redall[0]
        for i in range(1, count):
            total = total + redall[i]
        return finish_sum(total)

    precondition(vb, z1)
    loads[7].wait()
    operate(1, z1, w1)

    rhs = zero
    for c in range(nc):
        rhs = rhs + vw[c] * w1[c]
    sf[...] = rhs
    for side in range(2):
        sfp[side] = pack(rhs, side)
    mark = len(sent)
    for n, (dx, dy) in enumerate(SIDES):
        if dx:
            send(20 + n, sf, rfx.at[(1 - dx) // 2], dx, dy)
        else:
            send(20 + n, sfp.at[(1 + dy) // 2], rfy.at[(1 - dy) // 2], dx, dy)
    for n, (dx, dy) in enumerate(CORNERS):
        send(24 + n, sfp.at[(1 + dy) // 2], rfd.at[3 - n], dx, dy)
    group = sent[mark:]
    copies = start_lines([
        dot(lambda c: vb[c], lambda c: vb[c]),
        dot(lambda c: vb[c], lambda c: w1[c]),
        dot(lambda c: w1[c], lambda c: w1[c]),
    ])
    receive(group)
    for block in range(3):
        own = (rfx[0], sf[...], rfx[1])[block]
        left = (rfd[0], rfy[0], rfd[2])[block]
        right = (rfd[1], rfy[1], rfd[3])[block]
        fext[block * rows:(block + 1) * rows, 0:cols] = own
        fext[block * rows:(block + 1) * rows, cols:2 * cols] = unpack(left, right, 0.0)
    precondition(w1, q1)
    copies = turn_lines(copies)
    operate(2, q1, vout)

    bb, bw, ww = end_lines(copies)
    beta = jnp.sqrt(bb)
    h11 = bw / bb
    h21 = jnp.sqrt(ww / bb - h11 * h11)
    scale = 1.0 / (beta * h21)
    over = 1.0 / beta

    def mapped(c):
        return (vout[c] - h11 * w1[c]) * scale

    def basis2(c):
        return (w1[c] - h11 * vb[c]) * scale

    h12, h22, squared = reduce_all([
        dot(mapped, lambda c: vb[c] * over),
        dot(mapped, basis2),
        dot(mapped, mapped),
    ])
    h32 = jnp.sqrt(squared - h12 * h12 - h22 * h22)

    radius1 = jnp.sqrt(h11 * h11 + h21 * h21)
    cos1, sin1 = h11 / radius1, h21 / radius1
    top, low = cos1 * h12 + sin1 * h22, -sin1 * h12 + cos1 * h22
    radius2 = jnp.sqrt(low * low + h32 * h32)
    cos2, sin2 = low / radius2, h32 / radius2
    g0, g1 = cos1 * beta, -sin1 * beta
    g1, g2 = cos2 * g1, -sin2 * g1
    y2 = g1 / radius2
    y1 = (g0 - top * y2) / radius1
    est_ref[...] = jnp.abs(g2)
    second = y2 * scale
    first = y1 * over - second * h11
    for c in range(nc):
        out_hbm[c] = first * z1[c] + second * q1[c]

    for k, src, dst, dx, dy in sent:
        @pl.when(has[(dx, dy)])
        def _(k=k, src=src, dst=dst, dx=dx, dy=dy):
            describe(k, src, dst, dx, dy).wait_send()


def on_device(gx, gy, right_side, diag, couple, trans, weights, well):
    nc, rows, cols = right_side.shape
    f32 = jnp.float32
    wide = (3 * rows, 2 * cols)
    vm = lambda *shape: pltpu.VMEM(shape, f32)
    dma = lambda *shape: pltpu.SemaphoreType.DMA(shape)
    field = (nc, rows, cols)
    pad = -(-nc // 8) * 8
    out, est = pl.pallas_call(
        functools.partial(kernel, gx, gy),
        name="cpr_gmres",
        out_shape=(jax.ShapeDtypeStruct(field, f32), jax.ShapeDtypeStruct((1, 1), f32)),
        in_specs=[pl.BlockSpec(memory_space=pltpu.HBM)] * 6,
        out_specs=(pl.BlockSpec(memory_space=pltpu.VMEM), pl.BlockSpec(memory_space=pltpu.VMEM)),
        scratch_shapes=[
            vm(*field), vm(nc, *field), vm(nc, *field), vm(4, rows, cols), vm(*field),
            pltpu.VMEM((rows, cols), jnp.int32), vm(nc, *field), vm(4, *field),
            vm(*field), vm(*field), vm(*field), vm(*field),
            vm(3, 2, pad, cols), vm(3, 2, pad, cols), vm(3, 2, rows, cols), vm(3, 2, rows, cols),
            vm(6, rows, cols), vm(2, 6, 8, cols), vm(2, 6, rows, cols), vm(2, 6, 8, cols),
            vm(4, 6, 8, cols), vm(rows, cols), vm(2, 8, cols), vm(8, cols), vm(8, 8, cols),
            vm(4, rows, cols), vm(2, rows, cols), vm(2, 8, cols),
            vm(4, 8, cols),
            vm(5, *wide), vm(4, *wide), vm(4, *wide), vm(4, *wide), vm(4, *wide),
            vm(4, *wide), vm(3, *wide), vm(*wide), vm(*field),
            vm(3, 8, cols), vm(gy, 8, cols), vm(gx, 8, cols), vm(gx * gy, 8, cols),
            dma(8), dma(36), dma(36), dma(gy - 1), dma(gy - 1), dma(gx - 1), dma(gx - 1),
            dma(gx * gy - 1), dma(gx * gy - 1),
        ],
        compiler_params=pltpu.CompilerParams(
            collective_id=0, has_side_effects=True, vmem_limit_bytes=60 << 20),
    )(right_side, diag, couple, trans, weights, well)
    return out, est.reshape(())


def solution(mesh):
    return jax.shard_map(
        functools.partial(on_device, mesh.shape["gx"], mesh.shape["gy"]),
        mesh=mesh,
        in_specs=(
            P(None, "gx", "gy"),
            P(None, None, "gx", "gy"),
            P(None, None, "gx", "gy"),
            P(None, "gx", "gy"),
            P(None, "gx", "gy"),
            P("gx", "gy"),
        ),
        out_specs=(P(None, "gx", "gy"), P()),
        check_vma=False,
    )
```
